32 devices in a mesh: blocks: 8 (over z, core), lev: 4 (over y, x).
Axes of the slice: x: 2, y: 2, z: 4, core: 2. Of those that a mesh axis runs over, the one named last changes fastest.
Arguments:
- tracers: float32 [8, 4, 8, 128, 128], P('blocks', 'lev'), may hold values from -6 to 6
- east_velocity: float32 [8, 8, 128, 128], P('blocks'), may hold values from -0.24 to 0.24
- north_velocity: float32 [8, 8, 128, 128], P('blocks'), may hold values from -0.24 to 0.24
- upward_velocity: float32 [8, 8, 128, 128], P('blocks'), may hold values from -0.24 to 0.24
- target: float32 [8, 4, 8, 128, 128], P('blocks', 'lev'), may hold values from 0.09375 to 12.65625
- bottom: int32 [8, 128, 128], P('blocks'), may hold values from 0 to 8, as said below
- shave_fraction: float32 [8, 128, 128], P('blocks'), may hold values from 0.05 to 1, as said below
- side_bottom: int32 [8, 4, 128], P('blocks'), may hold values from 0 to 8, as said below
- neighbors: int32 [8, 4], P('blocks'), may hold values from -1 to 7, as said below
- fold_partner: int32 [8], P('blocks'), may hold values from -1 to 7, as said below
- thin_pairs: int32 [8, 2, 128], P('blocks'), may hold values from 0 to 16383, as said below
Outputs:
- new_tracers: float32 [8, 4, 8, 128, 128], P('blocks', 'lev')
The draws below stay inside these ranges and needn't reach their ends.
Inputs may be any that keep to these rules, and one draw needn't show every extreme that they name: The blocks form a grid of 3 block columns, periodic from west to east, and 4 block rows; entries are mutual: neighbors[b,0] = c exactly when neighbors[c,1] = b, and neighbors[b,2] = c exactly when neighbors[c,3] = b; a block's entries that are not -1 differ; blocks of the top row have -1 to the north. `fold_partner`: set exactly for the blocks of the top row; mutual, a block may be its own partner. `bottom`: every block has wet columns. `side_bottom`: equals the bottom of the adjacent column or row of the neighbouring block, across the north fold the partner's top row in reversed order, 0 where no block lies. `thin_pairs`: thin cells of a block are distinct and have bottom 1 or more; each partner is the cell just east of its thin cell in the same row, with a bottom no smaller; no cell appears twice in a block. `shave_fraction`: listed thin cells have 0.05 to 0.2, all other cells 0.5 to 1.
All inputs are finite; a program needn't handle non-finite values.
Results may differ from the reference program's by a relative error of at most 0.0003.
Values sent between devices are 32-bit elements; how exact they have to be, the bound alone decides.
A program may use at most 64 MiB of HBM per device.

```python
import math
import jax
import jax.numpy as jnp
from jax import lax

BS = 128
LEVELS = 8
NTHIN = 128
TRACERS = 4
GX = 3
GY = 4
N_BLOCKS = 8


def block_layout(key):
    layout_key = jax.random.fold_in(key, 11)
    inner = (GY - 1) * GX
    chosen = jax.random.permutation(jax.random.fold_in(layout_key, 1), inner)[:N_BLOCKS - GX]
    tiles = jnp.concatenate([chosen.astype(jnp.int32), inner + jnp.arange(GX, dtype=jnp.int32)])
    ordering = jax.random.permutation(jax.random.fold_in(layout_key, 2), N_BLOCKS)
    tile_of = tiles[ordering]
    block_of = jnp.full((GX * GY,), -1, jnp.int32).at[tile_of].set(jnp.arange(N_BLOCKS, dtype=jnp.int32))
    column = tile_of % GX
    row_index = tile_of // GX
    west = block_of[row_index * GX + (column + GX - 1) % GX]
    east = block_of[row_index * GX + (column + 1) % GX]
    south = jnp.where(row_index > 0, block_of[jnp.maximum(row_index - 1, 0) * GX + column], -1)
    north = jnp.where(row_index < GY - 1, block_of[jnp.minimum(row_index + 1, GY - 1) * GX + column], -1)
    mirror = jnp.where(row_index == GY - 1, block_of[row_index * GX + GX - 1 - column], -1)
    return (jnp.stack([west, east, south, north], 1).astype(jnp.int32), mirror.astype(jnp.int32))


def column_draw(key):
    column_key = jax.random.fold_in(key, 23)

    def one_block(index):
        block_key = jax.random.fold_in(column_key, index)
        threshold = jax.random.randint(jax.random.fold_in(block_key, 4), (), 1, 13)
        landing = jax.random.randint(jax.random.fold_in(block_key, 1), (BS * BS,), 0, 20) < threshold
        depth_draw = jax.random.randint(jax.random.fold_in(block_key, 2), (BS * BS,), 1, LEVELS + 1)
        levels_wet = jnp.where(landing, 0, depth_draw).astype(jnp.int32)
        thin_cells = (2 * jax.random.permutation(jax.random.fold_in(block_key, 3), BS * BS // 2)[:NTHIN]).astype(jnp.int32)
        partner = thin_cells + 1
        levels_wet = levels_wet.at[thin_cells].set(jnp.maximum(levels_wet[thin_cells], 1))
        levels_wet = levels_wet.at[partner].set(jnp.maximum(levels_wet[partner], levels_wet[thin_cells]))
        return (levels_wet, jnp.stack([thin_cells, partner]))
    return jax.vmap(one_block)(jnp.arange(N_BLOCKS, dtype=jnp.int32))


def draw_neighbors(key, part):
    return block_layout(key)[0]


def draw_fold_partner(key, part):
    return block_layout(key)[1]


def draw_bottom(key, part):
    return column_draw(key)[0].reshape(N_BLOCKS, BS, BS)


def draw_thin_pairs(key, part):
    return column_draw(key)[1]


def take_rows(edge, index):
    safe = jnp.maximum(index, 0)
    return jnp.where((index >= 0)[:, None], edge[safe], 0)


def draw_side_bottom(key, part):
    sides, mirror = block_layout(key)
    grid = column_draw(key)[0].reshape(N_BLOCKS, BS, BS)
    west = take_rows(grid[:, :, BS - 1], sides[:, 0])
    east = take_rows(grid[:, :, 0], sides[:, 1])
    south = take_rows(grid[:, BS - 1, :], sides[:, 2])
    north = take_rows(grid[:, 0, :], sides[:, 3]) + take_rows(grid[:, BS - 1, ::-1], mirror)
    return jnp.stack([west, east, south, north], 1).astype(jnp.int32)


def draw_shave_fraction(key, part):
    pairs = column_draw(key)[1]
    full_shape = (N_BLOCKS, BS * BS)
    unit_first = jax.random.uniform(jax.random.fold_in(key, 41), full_shape, jnp.float32)
    unit_second = jax.random.uniform(jax.random.fold_in(key, 42), full_shape, jnp.float32)
    regular = 0.5 + 0.5 * unit_first
    thin_value = 0.05 + 0.15 * unit_second
    marks = jnp.zeros(full_shape, jnp.int32).at[jnp.arange(N_BLOCKS)[:, None], pairs[:, 0]].set(1)
    return jnp.where(marks == 1, thin_value, regular).reshape(N_BLOCKS, BS, BS)


def draw_target(key, part):
    block_ramp = 0.5 + jnp.arange(N_BLOCKS, dtype=jnp.float32) / (N_BLOCKS - 1)
    tracer_ramp = 0.5 + jnp.arange(TRACERS, dtype=jnp.float32) / (TRACERS - 1)
    full_shape = (N_BLOCKS, TRACERS, LEVELS, BS, BS)
    block_unit = jax.random.uniform(jax.random.fold_in(key, 61), (N_BLOCKS,), jnp.float32)
    level_unit = jax.random.uniform(jax.random.fold_in(key, 62), (TRACERS, LEVELS), jnp.float32)
    cell_unit = jax.random.uniform(jax.random.fold_in(key, 63), full_shape, jnp.float32)
    block_scale = jnp.exp(math.log(3.0) * block_unit)
    level_scale = 0.75 + 0.5 * level_unit
    cell_scale = 0.5 + cell_unit
    outer = (block_ramp * block_scale)[:, None, None, None, None] * tracer_ramp[None, :, None, None, None]
    return outer * level_scale[None, :, :, None, None] * cell_scale


def steps_of(stream_key, extent, split, smallest, top_value):
    gain = 1.0
    for position, parts in split:
        heights = jax.random.uniform(jax.random.fold_in(jax.random.fold_in(stream_key, 6), position), (parts,), jnp.float32, smallest / len(split), top_value / len(split))
        gain = gain * jnp.repeat(jnp.exp(heights), extent[position] // parts).reshape((-1,) + (1,) * (len(extent) - 1 - position))
    return gain


def normal_values(key, dims, scale, limit, shards=(), held_as=jnp.bfloat16):
    array = jax.random.normal(key, dims, jnp.float32) * scale
    if len(shards) > 0:
        array = steps_of(key, dims, shards, -0.22, 0.18) * array
    return jnp.clip(array, min=-limit, max=limit).astype(held_as)


def setup_inputs(seed: int = 0) -> dict:
    key_list = jax.random.split(jax.random.key(seed), 12)
    return {
        "tracers": normal_values(key_list[0], (N_BLOCKS, TRACERS, LEVELS, BS, BS), 1.0, 6.0, ((0, 8), (1, 4)), jnp.float32),
        "east_velocity": jnp.clip(jax.random.uniform(key_list[1], (N_BLOCKS, LEVELS, BS, BS), jnp.float32, -0.24, 0.24) * steps_of(key_list[1], (N_BLOCKS, LEVELS, BS, BS), ((0, 8),), -0.4, 0.0), -0.24, 0.24),
        "north_velocity": jnp.clip(jax.random.uniform(key_list[2], (N_BLOCKS, LEVELS, BS, BS), jnp.float32, -0.24, 0.24) * steps_of(key_list[2], (N_BLOCKS, LEVELS, BS, BS), ((0, 8),), -0.4, 0.0), -0.24, 0.24),
        "upward_velocity": jnp.clip(jax.random.uniform(key_list[3], (N_BLOCKS, LEVELS, BS, BS), jnp.float32, -0.24, 0.24) * steps_of(key_list[3], (N_BLOCKS, LEVELS, BS, BS), ((0, 8),), -0.4, 0.0), -0.24, 0.24),
        "target": draw_target(jax.random.fold_in(key_list[11], 71), 0),
        "bottom": draw_bottom(jax.random.fold_in(key_list[11], 71), 0),
        "shave_fraction": draw_shave_fraction(jax.random.fold_in(key_list[11], 71), 0),
        "side_bottom": draw_side_bottom(jax.random.fold_in(key_list[11], 71), 0),
        "neighbors": draw_neighbors(jax.random.fold_in(key_list[11], 71), 0),
        "fold_partner": draw_fold_partner(jax.random.fold_in(key_list[11], 71), 0),
        "thin_pairs": draw_thin_pairs(jax.random.fold_in(key_list[11], 71), 0),
    }


RATE = 0.5


def upwind(face, first, second):
    return jnp.maximum(face, 0.0) * first + jnp.minimum(face, 0.0) * second


def column_masks(levels, bottom, shave_fraction):
    level_grid = levels[None, None, :, None, None]
    column_bottom = bottom[:, None, None]
    wet = level_grid < column_bottom
    thick = jnp.where(level_grid < column_bottom - 1, 1.0, jnp.where(level_grid == column_bottom - 1, shave_fraction[:, None, None], 0.0))
    return wet, thick


def level_pair(field):
    zero_level = jnp.zeros_like(field[:, :, :1])
    return jnp.concatenate([zero_level, field[:, :, :-1]], 2), jnp.concatenate([field[:, :, 1:], zero_level], 2)


def advected_field(tracers, east_flow, north_flow, upward_flow, levels, bottom, wet, thick, side_bottom, west_pair, east_pair, south_pair, north_pair):
    level_grid = levels[None, None, :, None, None]
    column_bottom = bottom[:, None, None]
    edge_levels = levels[None, None, :, None]
    wet_west = edge_levels < side_bottom[:, 0][:, None, None, :]
    wet_east = edge_levels < side_bottom[:, 1][:, None, None, :]
    wet_south = edge_levels < side_bottom[:, 2][:, None, None, :]
    wet_north = edge_levels < side_bottom[:, 3][:, None, None, :]
    east_values = jnp.concatenate([tracers[..., 1:], east_pair[0][..., None]], -1)
    east_flows = jnp.concatenate([east_flow[..., 1:], east_pair[1][..., None]], -1)
    east_wets = jnp.concatenate([wet[..., 1:], wet_east[..., None]], -1)
    flux_east = upwind(jnp.where(wet & east_wets, 0.5 * (east_flow + east_flows), 0.0), tracers, east_values)
    west_face = jnp.where(wet_west & wet[..., 0], 0.5 * (west_pair[1] + east_flow[..., 0]), 0.0)
    flux_west = jnp.concatenate([upwind(west_face, west_pair[0], tracers[..., 0])[..., None], flux_east[..., :-1]], -1)
    north_values = jnp.concatenate([tracers[..., 1:, :], north_pair[0][..., None, :]], -2)
    north_flows = jnp.concatenate([north_flow[..., 1:, :], north_pair[1][..., None, :]], -2)
    north_wets = jnp.concatenate([wet[..., 1:, :], wet_north[..., None, :]], -2)
    flux_north = upwind(jnp.where(wet & north_wets, 0.5 * (north_flow + north_flows), 0.0), tracers, north_values)
    south_face = jnp.where(wet_south & wet[..., 0, :], 0.5 * (south_pair[1] + north_flow[..., 0, :]), 0.0)
    flux_south = jnp.concatenate([upwind(south_face, south_pair[0], tracers[..., 0, :])[..., None, :], flux_north[..., :-1, :]], -2)
    above_values, below_values = level_pair(tracers)
    above_flow, below_flow = level_pair(upward_flow)
    wet_above = (level_grid >= 1) & (level_grid - 1 < column_bottom)
    wet_below = level_grid + 1 < column_bottom
    flux_lower = upwind(jnp.where(wet & wet_below, 0.5 * (upward_flow + below_flow), 0.0), below_values, tracers)
    flux_upper = upwind(jnp.where(wet & wet_above, 0.5 * (above_flow + upward_flow), 0.0), tracers, above_values)
    divergence = flux_west - flux_east + flux_south - flux_north + flux_lower - flux_upper
    return tracers + jnp.where(wet, divergence / jnp.where(wet, thick, 1.0), 0.0)


def merge_block(field, bottom, shave_fraction, pairs, levels):
    flat = field.reshape(field.shape[0], field.shape[1], -1)
    thin_cells = pairs[0]
    partner = pairs[1]
    depth_index = bottom[thin_cells] - 1
    thin_thick = shave_fraction[thin_cells]
    partner_thick = jnp.where(bottom[partner] - 1 == depth_index, shave_fraction[partner], 1.0)
    thin_values = flat[:, :, thin_cells]
    partner_values = flat[:, :, partner]
    merged = (thin_thick * thin_values + partner_thick * partner_values) / (thin_thick + partner_thick)
    struck = levels[:, None] == depth_index[None, :]
    flat = flat.at[:, :, thin_cells].set(jnp.where(struck, merged, thin_values))
    flat = flat.at[:, :, partner].set(jnp.where(struck, merged, partner_values))
    return flat.reshape(field.shape)


def pick(edge, index):
    safe = jnp.maximum(index, 0)
    present = (index >= 0).reshape((-1,) + (1,) * (edge.ndim - 1))
    return jnp.where(present, edge[safe], 0.0)


def reference(tracers, east_velocity, north_velocity, upward_velocity, target, bottom, shave_fraction, side_bottom, neighbors, fold_partner, thin_pairs):
    levels = jnp.arange(LEVELS, dtype=jnp.int32)
    east_flow = east_velocity[:, None]
    north_flow = north_velocity[:, None]
    west_values = pick(tracers[..., BS - 1], neighbors[:, 0])
    west_flows = pick(east_flow[..., BS - 1], neighbors[:, 0])
    east_values = pick(tracers[..., 0], neighbors[:, 1])
    east_flows = pick(east_flow[..., 0], neighbors[:, 1])
    south_values = pick(tracers[..., BS - 1, :], neighbors[:, 2])
    south_flows = pick(north_flow[..., BS - 1, :], neighbors[:, 2])
    north_values = pick(tracers[..., 0, :], neighbors[:, 3]) + pick(tracers[..., BS - 1, ::-1], fold_partner)
    north_flows = pick(north_flow[..., 0, :], neighbors[:, 3]) - pick(north_flow[..., BS - 1, ::-1], fold_partner)

    def block_totals(inputs):
        tracer_block, target_block, bottom_block, shave_block = inputs
        wet, thick = column_masks(levels, bottom_block[None], shave_block[None])
        restoring = RATE * (target_block[None] - tracer_block[None])
        return jnp.sum(jnp.where(wet, thick * restoring, 0.0)), jnp.sum(jnp.where(wet, thick, 0.0))

    sources, volumes = lax.map(block_totals, (tracers, target, bottom, shave_fraction))
    total_source = jnp.sum(sources)
    total_volume = TRACERS * jnp.sum(volumes)

    def block_step(inputs):
        (tracer_block, east_block, north_block, upward_block, target_block, bottom_block, shave_block, side_block, pairs_block,
         west_value, west_flow, east_value, east_flow_row, south_value, south_flow, north_value, north_flow_row) = inputs
        wet, thick = column_masks(levels, bottom_block[None], shave_block[None])
        tracer_one = tracer_block[None]
        advected = advected_field(tracer_one, east_block[None, None], north_block[None, None], upward_block[None, None], levels, bottom_block[None], wet, thick, side_block[None],
                                  (west_value[None], west_flow[None]), (east_value[None], east_flow_row[None]),
                                  (south_value[None], south_flow[None]), (north_value[None], north_flow_row[None]))
        restoring = RATE * (target_block[None] - tracer_one)
        stepped = jnp.where(wet, advected + restoring - total_source / total_volume, 0.0)
        return merge_block(stepped[0], bottom_block.reshape(-1), shave_block.reshape(-1), pairs_block, levels)

    return lax.map(block_step, (tracers, east_velocity, north_velocity, upward_velocity, target, bottom, shave_fraction, side_bottom, thin_pairs,
                                west_values, west_flows, east_values, east_flows, south_values, south_flows, north_values, north_flows))
```

```python
import functools

import jax
import jax.numpy as jnp
from jax import lax
from jax.experimental import pallas as pl
from jax.experimental.pallas import tpu as pltpu
from jax.sharding import PartitionSpec as P

RATE = 0.5
THIN_LIMIT = 0.35
MESH = pl.DeviceIdType.MESH
F32 = jnp.float32
HIGHEST = lax.Precision.HIGHEST


def upwind(face, first, second):
    return jnp.maximum(face, 0.0) * first + jnp.minimum(face, 0.0) * second


def kernel(
    nb,
    nl,
    nbr_hbm,
    fold_hbm,
    side_hbm,
    t_hbm,
    u_hbm,
    v_hbm,
    w_hbm,
    g_hbm,
    bottom_hbm,
    shave_hbm,
    out_ref,
    tg_ref,
    flow_ref,
    bottom_ref,
    shave_ref,
    nbr_ref,
    fold_ref,
    side_ref,
    x_ref,
    edge_ref,
    pick_ref,
    gain_ref,
    pay_ref,
    halo_ref,
    part_ref,
    parts_ref,
    in_sem,
    edge_send,
    edge_recv,
    part_send,
    part_recv,
):
    t_ref, g_ref = tg_ref.at[0], tg_ref.at[1]
    u_ref, v_ref, w_ref = (flow_ref.at[i] for i in range(3))
    levels, rows, cols = t_ref.shape
    n = nb * nl
    unroll = n <= 64
    block = lax.axis_index("blocks")
    lev = lax.axis_index("lev")
    late = (block >= nb // 2) & (lev > 0)

    def each_other(visit):
        def outer(i, carry):
            there = lax.rem(block + i, nb)

            def inner(j, carry):
                visit(i * nl + j - 1, {"blocks": there, "lev": lax.rem(lev + j, nl)})
                return carry

            return lax.fori_loop(0, nl, inner, carry, unroll=unroll)

        def first(j, carry):
            visit(j - 1, {"blocks": block, "lev": lax.rem(lev + j, nl)})
            return carry

        lax.fori_loop(1, nb, outer, 0, unroll=unroll)
        lax.fori_loop(1, nl, first, 0, unroll=unroll)

    plan = (
        (t_hbm, t_ref, 0),
        (bottom_hbm, bottom_ref, 1),
        (shave_hbm, shave_ref, 2),
        (g_hbm, g_ref, 0),
        (nbr_hbm, nbr_ref, 3),
        (fold_hbm, fold_ref, 4),
        (side_hbm, side_ref, 5),
        (u_hbm, u_ref, 6),
        (v_hbm, v_ref, 6),
        (w_hbm, w_ref, 6),
    )
    for src, dst, sem in plan:
        pltpu.make_async_copy(src, dst, in_sem.at[sem]).start()

    def arrived(ref, sem):
        pltpu.make_async_copy(ref, ref, in_sem.at[sem]).wait()

    barrier = pltpu.get_barrier_semaphore()

    each_other(
        lambda slot, device: pl.semaphore_signal(
            barrier, inc=1, device_id=device, device_id_type=MESH
        )
    )

    lane = lax.broadcasted_iota(jnp.int32, (rows, cols), 1)
    row = lax.broadcasted_iota(jnp.int32, (rows, cols), 0)
    lane_pair = lane // 2

    arrived(bottom_ref, 1)
    arrived(shave_ref, 2)
    arrived(tg_ref, 0)
    bottom = bottom_ref[...]
    shave = shave_ref[...]
    last = bottom - 1
    source = jnp.zeros((rows, cols), F32)
    for k in range(levels):
        thick = jnp.where(k < last, 1.0, jnp.where(k == last, shave, 0.0))
        source += thick * (RATE * (g_ref[k] - t_ref[k]))
    volume = jnp.where(bottom > 0, last.astype(F32) + shave, 0.0)
    source = jnp.sum(source, axis=0, keepdims=True)
    volume = jnp.sum(volume, axis=0, keepdims=True)
    half = cols // 2
    first_half = lax.broadcasted_iota(jnp.int32, (1, cols), 1) < half
    own_part = jnp.where(
        first_half,
        source + pltpu.roll(source, half, 1),
        volume + pltpu.roll(volume, half, 1),
    )
    part_ref[...] = own_part

    def send_parts():
        each_other(
            lambda slot, device: pltpu.make_async_remote_copy(
                src_ref=part_ref,
                dst_ref=parts_ref.at[slot],
                send_sem=part_send,
                recv_sem=part_recv,
                device_id=device,
                device_id_type=MESH,
            ).start()
        )

    @pl.when(late)
    def _():
        pl.semaphore_wait(barrier, n - 1)
        send_parts()

    def strip(fields):
        wide = jnp.zeros((rows, cols), F32)
        for j, field in enumerate(fields):
            wide = jnp.where(lane_pair == j, pltpu.roll(field(), 2 * j + 1, 1), wide)
        return wide.T

    arrived(flow_ref, 6)
    fields = [functools.partial(lambda k: t_ref[k], k) for k in range(levels)]
    fields += [functools.partial(lambda k: u_ref[k], k) for k in range(levels)]
    edge_ref[...] = strip(fields)
    t_east = edge_ref[pl.ds(0, levels, stride=2), :]
    t_west = edge_ref[pl.ds(1, levels, stride=2), :]
    u_east = edge_ref[pl.ds(2 * levels, levels, stride=2), :]
    u_west = edge_ref[pl.ds(2 * levels + 1, levels, stride=2), :]
    t_south = t_ref[:, 0, :]
    t_north = t_ref[:, rows - 1, :]
    v_south = v_ref[:, 0, :]
    v_north = v_ref[:, rows - 1, :]
    mirror = (
        lax.broadcasted_iota(jnp.int32, (cols, cols), 0)
        + lax.broadcasted_iota(jnp.int32, (cols, cols), 1)
        == cols - 1
    ).astype(F32)
    turned = jnp.dot(
        jnp.concatenate([t_north, v_north], 0), mirror, precision=HIGHEST, preferred_element_type=F32
    )
    t_edges = (t_west, t_east, t_south, t_north)
    f_edges = (u_west, u_east, v_south, v_north)
    arrived(nbr_ref, 3)
    arrived(fold_ref, 4)
    arrived(side_ref, 5)
    sides = [nbr_ref[0, s] for s in range(4)]
    fold = fold_ref[0, 0]
    blank = jnp.zeros((levels, cols), F32)

    def pack(i, carry):
        there = lax.rem(block + i, nb)
        t_side, f_side = blank, blank
        for s in range(4):
            hit = sides[s] == there
            t_side = jnp.where(hit, t_edges[s], t_side)
            f_side = jnp.where(hit, f_edges[s], f_side)
        pay_ref[i - 1, :levels, :] = t_side
        pay_ref[i - 1, levels : 2 * levels, :] = f_side
        pay_ref[i - 1, 2 * levels :, :] = turned
        return carry

    lax.fori_loop(1, nb, pack, 0, unroll=unroll)

    @pl.when(jnp.logical_not(late))
    def _():
        pl.semaphore_wait(barrier, n - 1)

    def send_edges(i, carry):
        pltpu.make_async_remote_copy(
            src_ref=pay_ref.at[i - 1],
            dst_ref=halo_ref.at[i - 1],
            send_sem=edge_send,
            recv_sem=edge_recv,
            device_id={"blocks": lax.rem(block + i, nb), "lev": lev},
            device_id_type=MESH,
        ).start()
        return carry

    lax.fori_loop(1, nb, send_edges, 0, unroll=unroll)

    @pl.when(jnp.logical_not(late))
    def _():
        send_parts()

    inverse = 1.0 / shave
    bottom_east = pltpu.roll(bottom, cols - 1, 1)
    open_east = jnp.where(lane == cols - 1, 0, jnp.minimum(bottom, bottom_east))
    open_north = jnp.where(row == rows - 1, 0, jnp.minimum(bottom, pltpu.roll(bottom, rows - 1, 0)))
    partner_shave = jnp.where(bottom_east == bottom, pltpu.roll(shave, cols - 1, 1), 1.0)
    scale = 1.0 / (shave + partner_shave)
    weight = shave * scale
    partner_weight = partner_shave * scale
    struck = jnp.where(shave < THIN_LIMIT, last, -1)
    struck_west = pltpu.roll(struck, 1, 1)

    edge_ref[...] = strip(
        (
            lambda: bottom.astype(F32),
            lambda: shave,
            lambda: jnp.where(lane == 0, weight, pltpu.roll(partner_weight, 1, 1)),
            lambda: jnp.where(lane == 0, struck, struck_west).astype(F32),
        )
    )

    upper = jnp.zeros((rows, cols), F32)
    for k in range(levels):
        t = t_ref[k]
        u = u_ref[k]
        v = v_ref[k]
        face = jnp.where(k < open_east, 0.5 * (u + pltpu.roll(u, cols - 1, 1)), 0.0)
        flux = upwind(face, t, pltpu.roll(t, cols - 1, 1))
        divergence = pltpu.roll(flux, 1, 1) - flux
        face = jnp.where(k < open_north, 0.5 * (v + pltpu.roll(v, rows - 1, 0)), 0.0)
        flux = upwind(face, t, pltpu.roll(t, rows - 1, 0))
        divergence += pltpu.roll(flux, 1, 0) - flux
        if k < levels - 1:
            face = jnp.where(k + 1 < bottom, 0.5 * (w_ref[k] + w_ref[k + 1]), 0.0)
            lower = upwind(face, t_ref[k + 1], t)
        else:
            lower = jnp.zeros((rows, cols), F32)
        divergence += lower - upper
        upper = lower
        x = t + divergence * jnp.where(k == last, inverse, 1.0) + RATE * (g_ref[k] - t)
        merged = weight * x + partner_weight * pltpu.roll(x, cols - 1, 1)
        x = jnp.where(struck == k, merged, x)
        x_ref[k] = jnp.where(struck_west == k, pltpu.roll(merged, 1, 1), x)

    places = (0, 1, cols - 2, cols - 1)
    kinds = len(places)
    source_row = lax.broadcasted_iota(jnp.int32, (kinds * levels, levels * cols), 0)
    target = lax.broadcasted_iota(jnp.int32, (kinds * levels, levels * cols), 1)
    chosen = jnp.zeros((kinds * levels, levels * cols), F32)
    for p, place in enumerate(places):
        chosen = jnp.where(target == (source_row - p * levels) * cols + place, 1.0, chosen)
    chosen = chosen.astype(jnp.bfloat16)
    for p in range(3):
        pick_ref[p * kinds * levels : (p + 1) * kinds * levels, :] = chosen

    grid = lax.broadcasted_iota(jnp.int32, (levels, cols), 0)
    grid_f = grid.astype(F32)
    edge_bottom = (
        edge_ref[1:2, :],
        edge_ref[0:1, :],
        bottom_ref[0:1, :].astype(F32),
        bottom_ref[rows - 1 : rows, :].astype(F32),
    )
    edge_shave = (
        edge_ref[3:4, :],
        edge_ref[2:3, :],
        shave_ref[0:1, :],
        shave_ref[rows - 1 : rows, :],
    )
    wets, scales = [], []
    for s in range(4):
        beyond = side_ref[s : s + 1, :].astype(F32)
        wets.append(grid_f < jnp.minimum(edge_bottom[s], beyond))
        scales.append(jnp.where(grid_f == edge_bottom[s] - 1.0, 1.0 / edge_shave[s], 1.0))
    side_weight = (edge_ref[5:6, :], edge_ref[4:5, :])
    side_struck = (edge_ref[7:8, :] == grid_f, edge_ref[6:7, :] == grid_f)

    found_t = [jnp.where(sides[s] == block, t_edges[s ^ 1], blank) for s in range(4)]
    found_f = [jnp.where(sides[s] == block, f_edges[s ^ 1], blank) for s in range(4)]
    hit = fold == block
    found_t[3] = jnp.where(hit, turned[:levels], found_t[3])
    found_f[3] = jnp.where(hit, -turned[levels:], found_f[3])

    pltpu.make_async_copy(halo_ref, halo_ref, edge_recv).wait()

    def collect(i, carry):
        found_t, found_f = list(carry[0]), list(carry[1])
        origin = lax.rem(block + nb - i, nb)
        side_t, side_f, over_t, over_f = (
            halo_ref[i - 1, p * levels : (p + 1) * levels, :] for p in range(4)
        )
        found_t = [jnp.where(sides[s] == origin, side_t, found_t[s]) for s in range(4)]
        found_f = [jnp.where(sides[s] == origin, side_f, found_f[s]) for s in range(4)]
        hit = fold == origin
        found_t[3] = jnp.where(hit, over_t, found_t[3])
        found_f[3] = jnp.where(hit, -over_f, found_f[3])
        return found_t, found_f

    found_t, found_f = lax.fori_loop(1, nb, collect, (found_t, found_f), unroll=unroll)

    gains = []
    for s in range(4):
        face = jnp.where(wets[s], 0.5 * (f_edges[s] + found_f[s]), 0.0)
        if s % 2 == 0:
            flux = upwind(face, found_t[s], t_edges[s])
        else:
            flux = -upwind(face, t_edges[s], found_t[s])
        gains.append(flux * scales[s])
    west = jnp.where(side_struck[0], side_weight[0] * gains[0], gains[0])
    east = jnp.where(side_struck[1], side_weight[1] * gains[1], gains[1])
    wide = jnp.concatenate(
        [
            west,
            jnp.where(side_struck[0], west, 0.0),
            jnp.where(side_struck[1], east, 0.0),
            east,
        ],
        0,
    )
    high = wide.astype(jnp.bfloat16)
    rest = wide - high.astype(F32)
    middle = rest.astype(jnp.bfloat16)
    low = (rest - middle.astype(F32)).astype(jnp.bfloat16)
    gain_ref[...] = lax.dot_general(
        jnp.concatenate([high, middle, low], 0),
        pick_ref[...],
        (((0,), (0,)), ((), ())),
        preferred_element_type=F32,
    )
    for s, r in ((2, 0), (3, rows - 1)):
        merged = weight[r : r + 1] * gains[s] + partner_weight[r : r + 1] * pltpu.roll(
            gains[s], cols - 1, 1
        )
        gain = jnp.where(struck[r : r + 1] == grid, merged, gains[s])
        gain = jnp.where(struck_west[r : r + 1] == grid, pltpu.roll(merged, 1, 1), gain)
        x_ref[:, r, :] += gain

    pltpu.make_async_copy(parts_ref, parts_ref, part_recv).wait()
    total = lax.fori_loop(
        0, n - 1, lambda i, carry: carry + parts_ref[i], part_ref[...], unroll=unroll
    )
    total_source = jnp.sum(jnp.where(first_half, total, 0.0), axis=1, keepdims=True)
    total_volume = jnp.sum(jnp.where(first_half, 0.0, total), axis=1, keepdims=True)
    mean = total_source / total_volume

    for k in range(levels):
        moved = x_ref[k] + gain_ref[:, k * cols : (k + 1) * cols]
        out_ref[k] = jnp.where(k < bottom_ref[...], moved - mean, 0.0)

    pltpu.make_async_copy(halo_ref, halo_ref, edge_send).wait()
    pltpu.make_async_copy(parts_ref, parts_ref, part_send).wait()


def local(
    nb,
    nl,
    tracers,
    east_velocity,
    north_velocity,
    upward_velocity,
    target,
    bottom,
    shave_fraction,
    side_bottom,
    neighbors,
    fold_partner,
    thin_pairs,
):
    levels, rows, cols = tracers.shape[2:]
    in_hbm = functools.partial(pltpu.with_memory_space_constraint, memory_space=pltpu.HBM)
    cube = (levels, rows, cols)
    n = nb * nl
    vmem = pl.BlockSpec(memory_space=pltpu.VMEM)
    grant = (14 << 20) + 4 * cols * (8 * levels * nb + 8 * n)
    anywhere = pl.BlockSpec(memory_space=pl.ANY)
    stepped = pl.pallas_call(
        functools.partial(kernel, nb, nl),
        out_shape=pltpu.VMEM(cube, F32),
        in_specs=[anywhere] * 10,
        out_specs=vmem,
        scratch_shapes=[
            pltpu.VMEM((2, *cube), F32),
            pltpu.VMEM((3, *cube), F32),
            pltpu.VMEM((rows, cols), jnp.int32),
            pltpu.VMEM((rows, cols), F32),
            pltpu.SMEM((1, 4), jnp.int32),
            pltpu.SMEM((1, 1), jnp.int32),
            pltpu.VMEM((4, cols), jnp.int32),
            pltpu.VMEM(cube, F32),
            pltpu.VMEM((cols, rows), F32),
            pltpu.VMEM((12 * levels, levels * cols), jnp.bfloat16),
            pltpu.VMEM((rows, levels * cols), F32),
            pltpu.VMEM((nb - 1, 4 * levels, cols), F32),
            pltpu.VMEM((nb - 1, 4 * levels, cols), F32),
            pltpu.VMEM((1, cols), F32),
            pltpu.VMEM((n - 1, 1, cols), F32),
            pltpu.SemaphoreType.DMA((7,)),
            pltpu.SemaphoreType.DMA,
            pltpu.SemaphoreType.DMA,
            pltpu.SemaphoreType.DMA,
            pltpu.SemaphoreType.DMA,
        ],
        compiler_params=pltpu.CompilerParams(
            collective_id=0, has_side_effects=True, vmem_limit_bytes=grant
        ),
    )(
        in_hbm(neighbors),
        fold_partner.reshape(1, 1),
        in_hbm(side_bottom.reshape(4, cols)),
        in_hbm(tracers.reshape(cube)),
        in_hbm(east_velocity.reshape(cube)),
        in_hbm(north_velocity.reshape(cube)),
        in_hbm(upward_velocity.reshape(cube)),
        in_hbm(target.reshape(cube)),
        in_hbm(bottom.reshape(rows, cols)),
        in_hbm(shave_fraction.reshape(rows, cols)),
    )
    return stepped.reshape(tracers.shape)


def solution(mesh):
    placed = (
        P("blocks", "lev", None, None, None),
        P("blocks", None, None, None),
        P("blocks", None, None, None),
        P("blocks", None, None, None),
        P("blocks", "lev", None, None, None),
        P("blocks", None, None),
        P("blocks", None, None),
        P("blocks", None, None),
        P("blocks", None),
        P("blocks"),
        P("blocks", None, None),
    )
    return jax.shard_map(
        functools.partial(local, mesh.shape["blocks"], mesh.shape["lev"]),
        mesh=mesh,
        in_specs=placed,
        out_specs=P("blocks", "lev", None, None, None),
        check_vma=False,
    )
```

```python
import functools

import jax
import jax.numpy as jnp
from jax import lax
from jax.experimental import pallas as pl
from jax.experimental.pallas import tpu as pltpu
from jax.sharding import PartitionSpec as P

RATE = 0.5
THIN_LIMIT = 0.35
MESH = pl.DeviceIdType.MESH
F32 = jnp.float32
HIGHEST = lax.Precision.HIGHEST


def upwind(face, first, second):
    return jnp.maximum(face, 0.0) * first + jnp.minimum(face, 0.0) * second


def kernel(
    nb,
    nl,
    nbr_hbm,
    fold_hbm,
    side_hbm,
    t_hbm,
    u_hbm,
    v_hbm,
    w_hbm,
    g_hbm,
    bottom_hbm,
    shave_hbm,
    out_ref,
    tg_ref,
    flow_ref,
    bottom_ref,
    shave_ref,
    nbr_ref,
    fold_ref,
    side_ref,
    x_ref,
    edge_ref,
    pick_ref,
    gain_ref,
    pay_ref,
    halo_ref,
    part_ref,
    sum_ref,
    column_ref,
    parts_ref,
    in_sem,
    edge_send,
    edge_recv,
    part_send,
    rest_send,
    column_recv,
    part_recv,
    ready,
):
    t_ref, g_ref = tg_ref.at[0], tg_ref.at[1]
    u_ref, v_ref, w_ref = (flow_ref.at[i] for i in range(3))
    levels, rows, cols = t_ref.shape
    n = nb * nl
    unroll = n <= 64
    block = lax.axis_index("blocks")
    lev = lax.axis_index("lev")
    late = (block >= nb // 2) & (lev > 0)

    first_column = lev == 0

    def each_block(visit, j, start):
        def along(i, carry):
            visit(i, {"blocks": lax.rem(block + i, nb), "lev": j})
            return carry

        lax.fori_loop(start, nb, along, 0, unroll=unroll)

    def to_rest(visit):
        for j in range(1, nl):
            each_block(visit, j, 1)

            @pl.when(lev != j)
            def _():
                visit(0, {"blocks": block, "lev": j})

    plan = (
        (t_hbm, t_ref, 0),
        (bottom_hbm, bottom_ref, 1),
        (shave_hbm, shave_ref, 2),
        (g_hbm, g_ref, 0),
        (nbr_hbm, nbr_ref, 3),
        (fold_hbm, fold_ref, 4),
        (side_hbm, side_ref, 5),
        (u_hbm, u_ref, 6),
        (v_hbm, v_ref, 6),
        (w_hbm, w_ref, 6),
    )
    for src, dst, sem in plan:
        pltpu.make_async_copy(src, dst, in_sem.at[sem]).start()

    def arrived(ref, sem):
        pltpu.make_async_copy(ref, ref, in_sem.at[sem]).wait()

    barrier = pltpu.get_barrier_semaphore()

    def signal(i, device):
        pl.semaphore_signal(barrier, inc=1, device_id=device, device_id_type=MESH)

    @pl.when(first_column)
    def _():
        each_block(signal, 0, 1)

    to_rest(signal)

    lane = lax.broadcasted_iota(jnp.int32, (rows, cols), 1)
    row = lax.broadcasted_iota(jnp.int32, (rows, cols), 0)
    lane_pair = lane // 2

    arrived(bottom_ref, 1)
    arrived(shave_ref, 2)
    arrived(tg_ref, 0)
    bottom = bottom_ref[...]
    shave = shave_ref[...]
    last = bottom - 1
    source = jnp.zeros((rows, cols), F32)
    for k in range(levels):
        thick = jnp.where(k < last, 1.0, jnp.where(k == last, shave, 0.0))
        source += thick * (RATE * (g_ref[k] - t_ref[k]))
    volume = jnp.where(bottom > 0, last.astype(F32) + shave, 0.0)
    source = jnp.sum(source, axis=0, keepdims=True)
    volume = jnp.sum(volume, axis=0, keepdims=True)
    half = cols // 2
    first_half = lax.broadcasted_iota(jnp.int32, (1, cols), 1) < half
    own_part = jnp.where(
        first_half,
        source + pltpu.roll(source, half, 1),
        volume + pltpu.roll(volume, half, 1),
    )
    part_ref[...] = own_part

    sum_ref[...] = own_part

    def send_row(src, dst, send, recv, device):
        pltpu.make_async_remote_copy(
            src_ref=src,
            dst_ref=dst,
            send_sem=send,
            recv_sem=recv,
            device_id=device,
            device_id_type=MESH,
        ).start()

    def meet():
        @pl.when(first_column)
        def _():
            pl.semaphore_wait(barrier, nb - 1)
            each_block(
                lambda i, device: send_row(
                    part_ref, column_ref.at[i - 1], part_send, column_recv, device
                ),
                0,
                1,
            )

        @pl.when(jnp.logical_not(first_column))
        def _():
            pl.semaphore_wait(barrier, n - 1)
            pl.semaphore_signal(
                ready, inc=1, device_id={"blocks": block, "lev": 0}, device_id_type=MESH
            )

            def send_part(send):
                return lambda i, device: send_row(
                    part_ref, parts_ref.at[(lev - 1) * nb + i], send, part_recv, device
                )

            each_block(send_part(part_send), 0, 0)
            to_rest(send_part(rest_send))

    @pl.when(late)
    def _():
        meet()

    def strip(fields):
        wide = jnp.zeros((rows, cols), F32)
        for j, field in enumerate(fields):
            wide = jnp.where(lane_pair == j, pltpu.roll(field(), 2 * j + 1, 1), wide)
        return wide.T

    arrived(flow_ref, 6)
    fields = [functools.partial(lambda k: t_ref[k], k) for k in range(levels)]
    fields += [functools.partial(lambda k: u_ref[k], k) for k in range(levels)]
    edge_ref[...] = strip(fields)
    t_east = edge_ref[pl.ds(0, levels, stride=2), :]
    t_west = edge_ref[pl.ds(1, levels, stride=2), :]
    u_east = edge_ref[pl.ds(2 * levels, levels, stride=2), :]
    u_west = edge_ref[pl.ds(2 * levels + 1, levels, stride=2), :]
    t_south = t_ref[:, 0, :]
    t_north = t_ref[:, rows - 1, :]
    v_south = v_ref[:, 0, :]
    v_north = v_ref[:, rows - 1, :]
    mirror = (
        lax.broadcasted_iota(jnp.int32, (cols, cols), 0)
        + lax.broadcasted_iota(jnp.int32, (cols, cols), 1)
        == cols - 1
    ).astype(F32)
    turned = jnp.dot(
        jnp.concatenate([t_north, v_north], 0), mirror, precision=HIGHEST, preferred_element_type=F32
    )
    t_edges = (t_west, t_east, t_south, t_north)
    f_edges = (u_west, u_east, v_south, v_north)
    arrived(nbr_ref, 3)
    arrived(fold_ref, 4)
    arrived(side_ref, 5)
    sides = [nbr_ref[0, s] for s in range(4)]
    fold = fold_ref[0, 0]
    blank = jnp.zeros((levels, cols), F32)

    def pack(i, carry):
        there = lax.rem(block + i, nb)
        t_side, f_side = blank, blank
        for s in range(4):
            hit = sides[s] == there
            t_side = jnp.where(hit, t_edges[s], t_side)
            f_side = jnp.where(hit, f_edges[s], f_side)
        pay_ref[i - 1, :levels, :] = t_side
        pay_ref[i - 1, levels : 2 * levels, :] = f_side
        pay_ref[i - 1, 2 * levels :, :] = turned
        return carry

    lax.fori_loop(1, nb, pack, 0, unroll=unroll)

    @pl.when(jnp.logical_not(late))
    def _():
        meet()

    def send_edges(i, carry):
        pltpu.make_async_remote_copy(
            src_ref=pay_ref.at[i - 1],
            dst_ref=halo_ref.at[i - 1],
            send_sem=edge_send,
            recv_sem=edge_recv,
            device_id={"blocks": lax.rem(block + i, nb), "lev": lev},
            device_id_type=MESH,
        ).start()
        return carry

    lax.fori_loop(1, nb, send_edges, 0, unroll=unroll)

    inverse = 1.0 / shave
    bottom_east = pltpu.roll(bottom, cols - 1, 1)
    open_east = jnp.where(lane == cols - 1, 0, jnp.minimum(bottom, bottom_east))
    open_north = jnp.where(row == rows - 1, 0, jnp.minimum(bottom, pltpu.roll(bottom, rows - 1, 0)))
    partner_shave = jnp.where(bottom_east == bottom, pltpu.roll(shave, cols - 1, 1), 1.0)
    scale = 1.0 / (shave + partner_shave)
    weight = shave * scale
    partner_weight = partner_shave * scale
    struck = jnp.where(shave < THIN_LIMIT, last, -1)
    struck_west = pltpu.roll(struck, 1, 1)

    edge_ref[...] = strip(
        (
            lambda: bottom.astype(F32),
            lambda: shave,
            lambda: jnp.where(lane == 0, weight, pltpu.roll(partner_weight, 1, 1)),
            lambda: jnp.where(lane == 0, struck, struck_west).astype(F32),
        )
    )

    upper = jnp.zeros((rows, cols), F32)
    for k in range(levels):
        t = t_ref[k]
        u = u_ref[k]
        v = v_ref[k]
        face = jnp.where(k < open_east, 0.5 * (u + pltpu.roll(u, cols - 1, 1)), 0.0)
        flux = upwind(face, t, pltpu.roll(t, cols - 1, 1))
        divergence = pltpu.roll(flux, 1, 1) - flux
        face = jnp.where(k < open_north, 0.5 * (v + pltpu.roll(v, rows - 1, 0)), 0.0)
        flux = upwind(face, t, pltpu.roll(t, rows - 1, 0))
        divergence += pltpu.roll(flux, 1, 0) - flux
        if k < levels - 1:
            face = jnp.where(k + 1 < bottom, 0.5 * (w_ref[k] + w_ref[k + 1]), 0.0)
            lower = upwind(face, t_ref[k + 1], t)
        else:
            lower = jnp.zeros((rows, cols), F32)
        divergence += lower - upper
        upper = lower
        x = t + divergence * jnp.where(k == last, inverse, 1.0) + RATE * (g_ref[k] - t)
        merged = weight * x + partner_weight * pltpu.roll(x, cols - 1, 1)
        x = jnp.where(struck == k, merged, x)
        x_ref[k] = jnp.where(struck_west == k, pltpu.roll(merged, 1, 1), x)

    places = (0, 1, cols - 2, cols - 1)
    kinds = len(places)
    source_row = lax.broadcasted_iota(jnp.int32, (kinds * levels, levels * cols), 0)
    target = lax.broadcasted_iota(jnp.int32, (kinds * levels, levels * cols), 1)
    chosen = jnp.zeros((kinds * levels, levels * cols), F32)
    for p, place in enumerate(places):
        chosen = jnp.where(target == (source_row - p * levels) * cols + place, 1.0, chosen)
    chosen = chosen.astype(jnp.bfloat16)
    for p in range(3):
        pick_ref[p * kinds * levels : (p + 1) * kinds * levels, :] = chosen

    grid = lax.broadcasted_iota(jnp.int32, (levels, cols), 0)
    grid_f = grid.astype(F32)
    edge_bottom = (
        edge_ref[1:2, :],
        edge_ref[0:1, :],
        bottom_ref[0:1, :].astype(F32),
        bottom_ref[rows - 1 : rows, :].astype(F32),
    )
    edge_shave = (
        edge_ref[3:4, :],
        edge_ref[2:3, :],
        shave_ref[0:1, :],
        shave_ref[rows - 1 : rows, :],
    )
    wets, scales = [], []
    for s in range(4):
        beyond = side_ref[s : s + 1, :].astype(F32)
        wets.append(grid_f < jnp.minimum(edge_bottom[s], beyond))
        scales.append(jnp.where(grid_f == edge_bottom[s] - 1.0, 1.0 / edge_shave[s], 1.0))
    side_weight = (edge_ref[5:6, :], edge_ref[4:5, :])
    side_struck = (edge_ref[7:8, :] == grid_f, edge_ref[6:7, :] == grid_f)

    found_t = [jnp.where(sides[s] == block, t_edges[s ^ 1], blank) for s in range(4)]
    found_f = [jnp.where(sides[s] == block, f_edges[s ^ 1], blank) for s in range(4)]
    hit = fold == block
    found_t[3] = jnp.where(hit, turned[:levels], found_t[3])
    found_f[3] = jnp.where(hit, -turned[levels:], found_f[3])

    @pl.when(first_column)
    def _():
        pltpu.make_async_copy(column_ref, column_ref, column_recv).wait()
        sum_ref[...] = part_ref[...] + jnp.sum(column_ref[...], axis=0)
        pl.semaphore_wait(ready, nl - 1)
        for j in range(1, nl):
            send_row(
                sum_ref,
                parts_ref.at[(j - 1) * nb],
                rest_send,
                part_recv,
                {"blocks": block, "lev": j},
            )

    pltpu.make_async_copy(halo_ref, halo_ref, edge_recv).wait()

    def collect(i, carry):
        found_t, found_f = list(carry[0]), list(carry[1])
        origin = lax.rem(block + nb - i, nb)
        side_t, side_f, over_t, over_f = (
            halo_ref[i - 1, p * levels : (p + 1) * levels, :] for p in range(4)
        )
        found_t = [jnp.where(sides[s] == origin, side_t, found_t[s]) for s in range(4)]
        found_f = [jnp.where(sides[s] == origin, side_f, found_f[s]) for s in range(4)]
        hit = fold == origin
        found_t[3] = jnp.where(hit, over_t, found_t[3])
        found_f[3] = jnp.where(hit, -over_f, found_f[3])
        return found_t, found_f

    found_t, found_f = lax.fori_loop(1, nb, collect, (found_t, found_f), unroll=unroll)

    gains = []
    for s in range(4):
        face = jnp.where(wets[s], 0.5 * (f_edges[s] + found_f[s]), 0.0)
        if s % 2 == 0:
            flux = upwind(face, found_t[s], t_edges[s])
        else:
            flux = -upwind(face, t_edges[s], found_t[s])
        gains.append(flux * scales[s])
    west = jnp.where(side_struck[0], side_weight[0] * gains[0], gains[0])
    east = jnp.where(side_struck[1], side_weight[1] * gains[1], gains[1])
    wide = jnp.concatenate(
        [
            west,
            jnp.where(side_struck[0], west, 0.0),
            jnp.where(side_struck[1], east, 0.0),
            east,
        ],
        0,
    )
    high = wide.astype(jnp.bfloat16)
    rest = wide - high.astype(F32)
    middle = rest.astype(jnp.bfloat16)
    low = (rest - middle.astype(F32)).astype(jnp.bfloat16)
    gain_ref[...] = lax.dot_general(
        jnp.concatenate([high, middle, low], 0),
        pick_ref[...],
        (((0,), (0,)), ((), ())),
        preferred_element_type=F32,
    )
    for s, r in ((2, 0), (3, rows - 1)):
        merged = weight[r : r + 1] * gains[s] + partner_weight[r : r + 1] * pltpu.roll(
            gains[s], cols - 1, 1
        )
        gain = jnp.where(struck[r : r + 1] == grid, merged, gains[s])
        gain = jnp.where(struck_west[r : r + 1] == grid, pltpu.roll(merged, 1, 1), gain)
        x_ref[:, r, :] += gain

    pltpu.make_async_copy(parts_ref, parts_ref, part_recv).wait()
    total = sum_ref[...] + jnp.sum(parts_ref[...], axis=0)
    total_source = jnp.sum(jnp.where(first_half, total, 0.0), axis=1, keepdims=True)
    total_volume = jnp.sum(jnp.where(first_half, 0.0, total), axis=1, keepdims=True)
    mean = total_source / total_volume

    for k in range(levels):
        moved = x_ref[k] + gain_ref[:, k * cols : (k + 1) * cols]
        out_ref[k] = jnp.where(k < bottom_ref[...], moved - mean, 0.0)

    pltpu.make_async_copy(halo_ref, halo_ref, edge_send).wait()

    def sent(ref, sem):
        pltpu.make_async_copy(ref, ref, sem).wait()

    @pl.when(first_column)
    def _():
        sent(column_ref, part_send)
        sent(parts_ref.at[: nl - 1], rest_send)

    @pl.when(jnp.logical_not(first_column))
    def _():
        sent(parts_ref.at[:nb], part_send)
        sent(parts_ref.at[: n - nb - 1], rest_send)


def local(
    nb,
    nl,
    tracers,
    east_velocity,
    north_velocity,
    upward_velocity,
    target,
    bottom,
    shave_fraction,
    side_bottom,
    neighbors,
    fold_partner,
    thin_pairs,
):
    levels, rows, cols = tracers.shape[2:]
    in_hbm = functools.partial(pltpu.with_memory_space_constraint, memory_space=pltpu.HBM)
    cube = (levels, rows, cols)
    n = nb * nl
    vmem = pl.BlockSpec(memory_space=pltpu.VMEM)
    grant = (14 << 20) + 4 * cols * (8 * levels * nb + 8 * n)
    anywhere = pl.BlockSpec(memory_space=pl.ANY)
    stepped = pl.pallas_call(
        functools.partial(kernel, nb, nl),
        out_shape=pltpu.VMEM(cube, F32),
        in_specs=[anywhere] * 10,
        out_specs=vmem,
        scratch_shapes=[
            pltpu.VMEM((2, *cube), F32),
            pltpu.VMEM((3, *cube), F32),
            pltpu.VMEM((rows, cols), jnp.int32),
            pltpu.VMEM((rows, cols), F32),
            pltpu.SMEM((1, 4), jnp.int32),
            pltpu.SMEM((1, 1), jnp.int32),
            pltpu.VMEM((4, cols), jnp.int32),
            pltpu.VMEM(cube, F32),
            pltpu.VMEM((cols, rows), F32),
            pltpu.VMEM((12 * levels, levels * cols), jnp.bfloat16),
            pltpu.VMEM((rows, levels * cols), F32),
            pltpu.VMEM((nb - 1, 4 * levels, cols), F32),
            pltpu.VMEM((nb - 1, 4 * levels, cols), F32),
            pltpu.VMEM((1, cols), F32),
            pltpu.VMEM((1, cols), F32),
            pltpu.VMEM((nb - 1, 1, cols), F32),
            pltpu.VMEM((n - nb, 1, cols), F32),
            pltpu.SemaphoreType.DMA((7,)),
            pltpu.SemaphoreType.DMA,
            pltpu.SemaphoreType.DMA,
            pltpu.SemaphoreType.DMA,
            pltpu.SemaphoreType.DMA,
            pltpu.SemaphoreType.DMA,
            pltpu.SemaphoreType.DMA,
            pltpu.SemaphoreType.REGULAR,
        ],
        compiler_params=pltpu.CompilerParams(
            collective_id=0, has_side_effects=True, vmem_limit_bytes=grant
        ),
    )(
        in_hbm(neighbors),
        fold_partner.reshape(1, 1),
        in_hbm(side_bottom.reshape(4, cols)),
        in_hbm(tracers.reshape(cube)),
        in_hbm(east_velocity.reshape(cube)),
        in_hbm(north_velocity.reshape(cube)),
        in_hbm(upward_velocity.reshape(cube)),
        in_hbm(target.reshape(cube)),
        in_hbm(bottom.reshape(rows, cols)),
        in_hbm(shave_fraction.reshape(rows, cols)),
    )
    return stepped.reshape(tracers.shape)


def solution(mesh):
    placed = (
        P("blocks", "lev", None, None, None),
        P("blocks", None, None, None),
        P("blocks", None, None, None),
        P("blocks", None, None, None),
        P("blocks", "lev", None, None, None),
        P("blocks", None, None),
        P("blocks", None, None),
        P("blocks", None, None),
        P("blocks", None),
        P("blocks"),
        P("blocks", None, None),
    )
    return jax.shard_map(
        functools.partial(local, mesh.shape["blocks"], mesh.shape["lev"]),
        mesh=mesh,
        in_specs=placed,
        out_specs=P("blocks", "lev", None, None, None),
        check_vma=False,
    )
```

```python
import functools

import jax
import jax.numpy as jnp
from jax import lax
from jax.experimental import pallas as pl
from jax.experimental.pallas import tpu as pltpu
from jax.sharding import PartitionSpec as P

RATE = 0.5
THIN_LIMIT = 0.35
MESH = pl.DeviceIdType.MESH
F32 = jnp.float32
HIGHEST = lax.Precision.HIGHEST


def upwind(face, first, second):
    return jnp.maximum(face, 0.0) * first + jnp.minimum(face, 0.0) * second


def kernel(
    nb,
    nl,
    nbr_hbm,
    fold_hbm,
    side_hbm,
    t_hbm,
    u_hbm,
    v_hbm,
    w_hbm,
    g_hbm,
    bottom_hbm,
    shave_hbm,
    x_ref,
    gain_ref,
    mean_ref,
    bottom_ref,
    tg_ref,
    flow_ref,
    shave_ref,
    nbr_ref,
    fold_ref,
    side_ref,
    edge_ref,
    own_ref,
    pick_ref,
    pay_ref,
    halo_ref,
    part_ref,
    sum_ref,
    column_ref,
    parts_ref,
    in_sem,
    edge_send,
    edge_recv,
    part_send,
    rest_send,
    column_recv,
    part_recv,
    ready,
):
    t_ref, g_ref = tg_ref.at[0], tg_ref.at[1]
    u_ref, v_ref, w_ref = (flow_ref.at[i] for i in range(3))
    levels, rows, cols = t_ref.shape
    n = nb * nl
    unroll = n <= 64
    block = lax.axis_index("blocks")
    lev = lax.axis_index("lev")
    far = block >= nb // 2
    late = far & (lev > 0)

    first_column = lev == 0

    def each_block(visit, j, start):
        def along(i, carry):
            visit(i, {"blocks": lax.rem(block + i, nb), "lev": j})
            return carry

        lax.fori_loop(start, nb, along, 0, unroll=unroll)

    def to_rest(visit):
        for j in range(1, nl):
            each_block(visit, j, 1)

            @pl.when(lev != j)
            def _():
                visit(0, {"blocks": block, "lev": j})

    def load(src, dst, sem):
        pltpu.make_async_copy(src, dst, in_sem.at[sem]).start()

    def load_flow():
        load(u_hbm, u_ref, 6)
        load(v_hbm, v_ref, 6)

    load(t_hbm, t_ref, 0)

    @pl.when(first_column)
    def _():
        load_flow()

    load(bottom_hbm, bottom_ref, 1)
    load(shave_hbm, shave_ref, 2)
    load(g_hbm, g_ref, 7)
    load(nbr_hbm, nbr_ref, 3)
    load(fold_hbm, fold_ref, 4)
    load(side_hbm, side_ref, 5)

    @pl.when(first_column)
    def _():
        load(w_hbm, w_ref, 8)

    def arrived(ref, sem):
        pltpu.make_async_copy(ref, ref, in_sem.at[sem]).wait()

    barrier = pltpu.get_barrier_semaphore()

    def signal(i, device):
        pl.semaphore_signal(barrier, inc=1, device_id=device, device_id_type=MESH)

    @pl.when(first_column)
    def _():
        each_block(signal, 0, 1)

    to_rest(signal)

    lane = lax.broadcasted_iota(jnp.int32, (rows, cols), 1)
    row = lax.broadcasted_iota(jnp.int32, (rows, cols), 0)
    lane_pair = lane // 2

    blank = jnp.zeros((levels, cols), F32)

    def strip(fields):
        wide = jnp.zeros((rows, cols), F32)
        for j, field in enumerate(fields):
            wide = jnp.where(lane_pair == j, pltpu.roll(field(), 2 * j + 1, 1), wide)
        return wide.T

    def pack_edges():
        fields = [functools.partial(lambda k: t_ref[k], k) for k in range(levels)]
        fields += [functools.partial(lambda k: u_ref[k], k) for k in range(levels)]
        edge_ref[...] = strip(fields)
        t_north = t_ref[:, rows - 1, :]
        v_north = v_ref[:, rows - 1, :]
        t_edges = (
            edge_ref[pl.ds(1, levels, stride=2), :],
            edge_ref[pl.ds(0, levels, stride=2), :],
            t_ref[:, 0, :],
            t_north,
        )
        f_edges = (
            edge_ref[pl.ds(2 * levels + 1, levels, stride=2), :],
            edge_ref[pl.ds(2 * levels, levels, stride=2), :],
            v_ref[:, 0, :],
            v_north,
        )
        mirror = (
            lax.broadcasted_iota(jnp.int32, (cols, cols), 0)
            + lax.broadcasted_iota(jnp.int32, (cols, cols), 1)
            == cols - 1
        ).astype(F32)
        turned = jnp.dot(
            jnp.concatenate([t_north, v_north], 0),
            mirror,
            precision=HIGHEST,
            preferred_element_type=F32,
        )
        for s in range(4):
            own_ref[s] = t_edges[s]
            own_ref[4 + s] = f_edges[s]
        own_ref[8] = turned[:levels]
        own_ref[9] = turned[levels:]
        arrived(nbr_ref, 3)
        sides = [nbr_ref[0, s] for s in range(4)]

        def pack(i, carry):
            there = lax.rem(block + i, nb)
            t_side, f_side = blank, blank
            for s in range(4):
                hit = sides[s] == there
                t_side = jnp.where(hit, t_edges[s], t_side)
                f_side = jnp.where(hit, f_edges[s], f_side)
            pay_ref[i - 1, :levels, :] = t_side
            pay_ref[i - 1, levels : 2 * levels, :] = f_side
            pay_ref[i - 1, 2 * levels :, :] = turned
            return carry

        lax.fori_loop(1, nb, pack, 0, unroll=unroll)

    def send_edges():
        def send(i, carry):
            pltpu.make_async_remote_copy(
                src_ref=pay_ref.at[i - 1],
                dst_ref=halo_ref.at[i - 1],
                send_sem=edge_send,
                recv_sem=edge_recv,
                device_id={"blocks": lax.rem(block + i, nb), "lev": lev},
                device_id_type=MESH,
            ).start()
            return carry

        lax.fori_loop(1, nb, send, 0, unroll=unroll)

    arrived(t_ref, 0)

    @pl.when(first_column)
    def _():
        arrived(flow_ref.at[:2], 6)
        pack_edges()

    @pl.when(first_column & (block > nb))
    def _():
        pl.semaphore_wait(barrier, nb - 1)
        send_edges()

    arrived(bottom_ref, 1)
    arrived(shave_ref, 2)
    arrived(g_ref, 7)

    @pl.when(jnp.logical_not(first_column))
    def _():
        load_flow()
        load(w_hbm, w_ref, 8)

    bottom = bottom_ref[...]
    shave = shave_ref[...]
    last = bottom - 1
    volume = jnp.where(bottom > 0, last.astype(F32) + shave, 0.0)
    source = jnp.clip(volume, 0.0, 1.0) * (g_ref[0] - t_ref[0])
    for k in range(1, levels):
        source += jnp.clip(volume - k, 0.0, 1.0) * (g_ref[k] - t_ref[k])
    source = RATE * jnp.sum(source, axis=0, keepdims=True)
    volume = jnp.sum(volume, axis=0, keepdims=True)
    half = cols // 2
    first_half = lax.broadcasted_iota(jnp.int32, (1, cols), 1) < half
    own_part = jnp.where(
        first_half,
        source + pltpu.roll(source, half, 1),
        volume + pltpu.roll(volume, half, 1),
    )
    part_ref[...] = own_part

    sum_ref[...] = own_part

    def send_row(src, dst, send, recv, device):
        pltpu.make_async_remote_copy(
            src_ref=src,
            dst_ref=dst,
            send_sem=send,
            recv_sem=recv,
            device_id=device,
            device_id_type=MESH,
        ).start()

    def meet():
        @pl.when(first_column)
        def _():
            @pl.when(block <= nb)
            def _():
                pl.semaphore_wait(barrier, nb - 1)

            each_block(
                lambda i, device: send_row(
                    part_ref, column_ref.at[i - 1], part_send, column_recv, device
                ),
                0,
                1,
            )

        @pl.when(jnp.logical_not(first_column))
        def _():
            pl.semaphore_wait(barrier, n - 1)
            pl.semaphore_signal(
                ready, inc=1, device_id={"blocks": block, "lev": 0}, device_id_type=MESH
            )

            def send_part(send):
                return lambda i, device: send_row(
                    part_ref, parts_ref.at[(lev - 1) * nb + i], send, part_recv, device
                )

            each_block(send_part(part_send), 0, 0)
            to_rest(send_part(rest_send))

    @pl.when(late)
    def _():
        meet()

    @pl.when(jnp.logical_not(first_column))
    def _():
        arrived(flow_ref.at[:2], 6)
        pack_edges()

    @pl.when(jnp.logical_not(late))
    def _():
        meet()

    @pl.when(block <= nb)
    def _():
        send_edges()

    arrived(w_ref, 8)
    arrived(fold_ref, 4)
    arrived(side_ref, 5)
    t_edges = [own_ref[s] for s in range(4)]
    f_edges = [own_ref[4 + s] for s in range(4)]
    turned_t, turned_f = own_ref[8], own_ref[9]
    sides = [nbr_ref[0, s] for s in range(4)]
    fold = fold_ref[0, 0]

    inverse = 1.0 / shave
    bottom_east = pltpu.roll(bottom, cols - 1, 1)
    open_east = jnp.where(lane == cols - 1, 0, jnp.minimum(bottom, bottom_east))
    open_north = jnp.where(row == rows - 1, 0, jnp.minimum(bottom, pltpu.roll(bottom, rows - 1, 0)))
    partner_shave = jnp.where(bottom_east == bottom, pltpu.roll(shave, cols - 1, 1), 1.0)
    scale = 1.0 / (shave + partner_shave)
    weight = shave * scale
    partner_weight = partner_shave * scale
    struck = jnp.where(shave < THIN_LIMIT, last, -1)
    struck_west = pltpu.roll(struck, 1, 1)

    edge_ref[...] = strip(
        (
            lambda: bottom.astype(F32),
            lambda: shave,
            lambda: jnp.where(lane == 0, weight, pltpu.roll(partner_weight, 1, 1)),
            lambda: jnp.where(lane == 0, struck, struck_west).astype(F32),
        )
    )

    upper = jnp.zeros((rows, cols), F32)
    for k in range(levels):
        t = t_ref[k]
        u = u_ref[k]
        v = v_ref[k]
        face = jnp.where(k < open_east, 0.5 * (u + pltpu.roll(u, cols - 1, 1)), 0.0)
        flux = upwind(face, t, pltpu.roll(t, cols - 1, 1))
        divergence = pltpu.roll(flux, 1, 1) - flux
        face = jnp.where(k < open_north, 0.5 * (v + pltpu.roll(v, rows - 1, 0)), 0.0)
        flux = upwind(face, t, pltpu.roll(t, rows - 1, 0))
        divergence += pltpu.roll(flux, 1, 0) - flux
        if k < levels - 1:
            face = jnp.where(k + 1 < bottom, 0.5 * (w_ref[k] + w_ref[k + 1]), 0.0)
            lower = upwind(face, t_ref[k + 1], t)
        else:
            lower = jnp.zeros((rows, cols), F32)
        divergence += lower - upper
        upper = lower
        x = t + divergence * jnp.where(k == last, inverse, 1.0) + RATE * (g_ref[k] - t)
        merged = weight * x + partner_weight * pltpu.roll(x, cols - 1, 1)
        x = jnp.where(struck == k, merged, x)
        x_ref[k] = jnp.where(struck_west == k, pltpu.roll(merged, 1, 1), x)

    places = (0, 1, cols - 2, cols - 1)
    kinds = len(places)
    source_row = lax.broadcasted_iota(jnp.int32, (kinds * levels, levels * cols), 0)
    target = lax.broadcasted_iota(jnp.int32, (kinds * levels, levels * cols), 1)
    chosen = jnp.zeros((kinds * levels, levels * cols), F32)
    for p, place in enumerate(places):
        chosen = jnp.where(target == (source_row - p * levels) * cols + place, 1.0, chosen)
    chosen = chosen.astype(jnp.bfloat16)
    for p in range(3):
        pick_ref[p * kinds * levels : (p + 1) * kinds * levels, :] = chosen

    grid = lax.broadcasted_iota(jnp.int32, (levels, cols), 0)
    grid_f = grid.astype(F32)
    edge_bottom = (
        edge_ref[1:2, :],
        edge_ref[0:1, :],
        bottom_ref[0:1, :].astype(F32),
        bottom_ref[rows - 1 : rows, :].astype(F32),
    )
    edge_shave = (
        edge_ref[3:4, :],
        edge_ref[2:3, :],
        shave_ref[0:1, :],
        shave_ref[rows - 1 : rows, :],
    )
    wets, scales = [], []
    for s in range(4):
        beyond = side_ref[s : s + 1, :].astype(F32)
        wets.append(grid_f < jnp.minimum(edge_bottom[s], beyond))
        scales.append(jnp.where(grid_f == edge_bottom[s] - 1.0, 1.0 / edge_shave[s], 1.0))
    side_weight = (edge_ref[5:6, :], edge_ref[4:5, :])
    side_struck = (edge_ref[7:8, :] == grid_f, edge_ref[6:7, :] == grid_f)

    found_t = [jnp.where(sides[s] == block, t_edges[s ^ 1], blank) for s in range(4)]
    found_f = [jnp.where(sides[s] == block, f_edges[s ^ 1], blank) for s in range(4)]
    hit = fold == block
    found_t[3] = jnp.where(hit, turned_t, found_t[3])
    found_f[3] = jnp.where(hit, -turned_f, found_f[3])

    @pl.when(first_column)
    def _():
        pltpu.make_async_copy(column_ref, column_ref, column_recv).wait()
        sum_ref[...] = part_ref[...] + jnp.sum(column_ref[...], axis=0)
        pl.semaphore_wait(ready, nl - 1)
        for j in range(1, nl):
            send_row(
                sum_ref,
                parts_ref.at[(j - 1) * nb],
                rest_send,
                part_recv,
                {"blocks": block, "lev": j},
            )

    pltpu.make_async_copy(halo_ref, halo_ref, edge_recv).wait()

    def collect(i, carry):
        found_t, found_f = list(carry[0]), list(carry[1])
        origin = lax.rem(block + nb - i, nb)
        side_t, side_f, over_t, over_f = (
            halo_ref[i - 1, p * levels : (p + 1) * levels, :] for p in range(4)
        )
        found_t = [jnp.where(sides[s] == origin, side_t, found_t[s]) for s in range(4)]
        found_f = [jnp.where(sides[s] == origin, side_f, found_f[s]) for s in range(4)]
        hit = fold == origin
        found_t[3] = jnp.where(hit, over_t, found_t[3])
        found_f[3] = jnp.where(hit, -over_f, found_f[3])
        return found_t, found_f

    found_t, found_f = lax.fori_loop(1, nb, collect, (found_t, found_f), unroll=unroll)

    gains = []
    for s in range(4):
        face = jnp.where(wets[s], 0.5 * (f_edges[s] + found_f[s]), 0.0)
        if s % 2 == 0:
            flux = upwind(face, found_t[s], t_edges[s])
        else:
            flux = -upwind(face, t_edges[s], found_t[s])
        gains.append(flux * scales[s])
    west = jnp.where(side_struck[0], side_weight[0] * gains[0], gains[0])
    east = jnp.where(side_struck[1], side_weight[1] * gains[1], gains[1])
    wide = jnp.concatenate(
        [
            west,
            jnp.where(side_struck[0], west, 0.0),
            jnp.where(side_struck[1], east, 0.0),
            east,
        ],
        0,
    )
    high = wide.astype(jnp.bfloat16)
    rest = wide - high.astype(F32)
    middle = rest.astype(jnp.bfloat16)
    low = (rest - middle.astype(F32)).astype(jnp.bfloat16)
    gain_ref[...] = lax.dot_general(
        jnp.concatenate([high, middle, low], 0),
        pick_ref[...],
        (((0,), (0,)), ((), ())),
        preferred_element_type=F32,
    )
    for s, r in ((2, 0), (3, rows - 1)):
        merged = weight[r : r + 1] * gains[s] + partner_weight[r : r + 1] * pltpu.roll(
            gains[s], cols - 1, 1
        )
        gain = jnp.where(struck[r : r + 1] == grid, merged, gains[s])
        gain = jnp.where(struck_west[r : r + 1] == grid, pltpu.roll(merged, 1, 1), gain)
        x_ref[:, r, :] += gain

    pltpu.make_async_copy(parts_ref, parts_ref, part_recv).wait()
    total = sum_ref[...] + jnp.sum(parts_ref[...], axis=0)
    total_source = jnp.sum(jnp.where(first_half, total, 0.0), axis=1, keepdims=True)
    total_volume = jnp.sum(jnp.where(first_half, 0.0, total), axis=1, keepdims=True)
    mean_ref[...] = jnp.broadcast_to(total_source / total_volume, (1, cols))

    pltpu.make_async_copy(halo_ref, halo_ref, edge_send).wait()

    def sent(ref, sem):
        pltpu.make_async_copy(ref, ref, sem).wait()

    @pl.when(first_column)
    def _():
        sent(column_ref, part_send)
        sent(parts_ref.at[: nl - 1], rest_send)

    @pl.when(jnp.logical_not(first_column))
    def _():
        sent(parts_ref.at[:nb], part_send)
        sent(parts_ref.at[: n - nb - 1], rest_send)


def finish(x_ref, gain_ref, mean_ref, bottom_ref, out_hbm, held_ref, sem):
    levels, _, cols = x_ref.shape
    mean = mean_ref[...]
    for k in range(levels):
        moved = x_ref[k] + gain_ref[:, k * cols : (k + 1) * cols]
        held_ref[k] = jnp.where(k < bottom_ref[...], moved - mean, 0.0)
        pltpu.make_async_copy(held_ref.at[k], out_hbm.at[k], sem).start()
    pltpu.make_async_copy(held_ref, held_ref, sem).wait()


def local(
    nb,
    nl,
    tracers,
    east_velocity,
    north_velocity,
    upward_velocity,
    target,
    bottom,
    shave_fraction,
    side_bottom,
    neighbors,
    fold_partner,
    thin_pairs,
):
    levels, rows, cols = tracers.shape[2:]
    in_hbm = functools.partial(pltpu.with_memory_space_constraint, memory_space=pltpu.HBM)
    cube = (levels, rows, cols)
    n = nb * nl
    vmem = pl.BlockSpec(memory_space=pltpu.VMEM)
    grant = (14 << 20) + 4 * cols * (8 * levels * nb + 8 * n)
    anywhere = pl.BlockSpec(memory_space=pl.ANY)
    kept = pl.pallas_call(
        functools.partial(kernel, nb, nl),
        out_shape=(
            pltpu.VMEM(cube, F32),
            pltpu.VMEM((rows, levels * cols), F32),
            pltpu.VMEM((1, cols), F32),
            pltpu.VMEM((rows, cols), jnp.int32),
        ),
        in_specs=[anywhere] * 10,
        out_specs=(vmem,) * 4,
        scratch_shapes=[
            pltpu.VMEM((2, *cube), F32),
            pltpu.VMEM((3, *cube), F32),
            pltpu.VMEM((rows, cols), F32),
            pltpu.SMEM((1, 4), jnp.int32),
            pltpu.SMEM((1, 1), jnp.int32),
            pltpu.VMEM((4, cols), jnp.int32),
            pltpu.VMEM((cols, rows), F32),
            pltpu.VMEM((10, levels, cols), F32),
            pltpu.VMEM((12 * levels, levels * cols), jnp.bfloat16),
            pltpu.VMEM((nb - 1, 4 * levels, cols), F32),
            pltpu.VMEM((nb - 1, 4 * levels, cols), F32),
            pltpu.VMEM((1, cols), F32),
            pltpu.VMEM((1, cols), F32),
            pltpu.VMEM((nb - 1, 1, cols), F32),
            pltpu.VMEM((n - nb, 1, cols), F32),
            pltpu.SemaphoreType.DMA((9,)),
            pltpu.SemaphoreType.DMA,
            pltpu.SemaphoreType.DMA,
            pltpu.SemaphoreType.DMA,
            pltpu.SemaphoreType.DMA,
            pltpu.SemaphoreType.DMA,
            pltpu.SemaphoreType.DMA,
            pltpu.SemaphoreType.REGULAR,
        ],
        compiler_params=pltpu.CompilerParams(
            collective_id=0, has_side_effects=True, vmem_limit_bytes=grant
        ),
    )(
        in_hbm(neighbors),
        fold_partner.reshape(1, 1),
        in_hbm(side_bottom.reshape(4, cols)),
        in_hbm(tracers.reshape(cube)),
        in_hbm(east_velocity.reshape(cube)),
        in_hbm(north_velocity.reshape(cube)),
        in_hbm(upward_velocity.reshape(cube)),
        in_hbm(target.reshape(cube)),
        in_hbm(bottom.reshape(rows, cols)),
        in_hbm(shave_fraction.reshape(rows, cols)),
    )
    stepped = pl.pallas_call(
        finish,
        out_shape=pltpu.HBM(cube, F32),
        in_specs=[vmem] * 4,
        out_specs=anywhere,
        scratch_shapes=[pltpu.VMEM(cube, F32), pltpu.SemaphoreType.DMA],
        compiler_params=pltpu.CompilerParams(vmem_limit_bytes=2 << 20),
    )(*kept)
    return stepped.reshape(tracers.shape)


def solution(mesh):
    placed = (
        P("blocks", "lev", None, None, None),
        P("blocks", None, None, None),
        P("blocks", None, None, None),
        P("blocks", None, None, None),
        P("blocks", "lev", None, None, None),
        P("blocks", None, None),
        P("blocks", None, None),
        P("blocks", None, None),
        P("blocks", None),
        P("blocks"),
        P("blocks", None, None),
    )
    return jax.shard_map(
        functools.partial(local, mesh.shape["blocks"], mesh.shape["lev"]),
        mesh=mesh,
        in_specs=placed,
        out_specs=P("blocks", "lev", None, None, None),
        check_vma=False,
    )
```

```python
import functools

import jax
import jax.numpy as jnp
from jax import lax
from jax.experimental import pallas as pl
from jax.experimental.pallas import tpu as pltpu
from jax.sharding import PartitionSpec as P

RATE = 0.5
THIN_LIMIT = 0.35
MESH = pl.DeviceIdType.MESH
F32 = jnp.float32
HIGHEST = lax.Precision.HIGHEST


def upwind(face, first, second):
    return jnp.maximum(face, 0.0) * first + jnp.minimum(face, 0.0) * second


def kernel(
    nb,
    nl,
    nbr_hbm,
    fold_hbm,
    side_hbm,
    t_hbm,
    u_hbm,
    v_hbm,
    w_hbm,
    g_hbm,
    bottom_hbm,
    shave_hbm,
    x_ref,
    mean_ref,
    bottom_ref,
    tg_ref,
    flow_ref,
    shave_ref,
    nbr_ref,
    fold_ref,
    side_ref,
    edge_ref,
    own_ref,
    pick_ref,
    pay_ref,
    halo_ref,
    part_ref,
    sum_ref,
    column_ref,
    parts_ref,
    in_sem,
    edge_send,
    edge_recv,
    part_send,
    rest_send,
    column_recv,
    part_recv,
    ready,
):
    t_ref, g_ref = tg_ref.at[0], tg_ref.at[1]
    u_ref, v_ref, w_ref = (flow_ref.at[i] for i in range(3))
    levels, rows, cols = t_ref.shape
    n = nb * nl
    unroll = n <= 64
    block = lax.axis_index("blocks")
    lev = lax.axis_index("lev")
    far = block >= nb // 2

    first_column = lev == 0

    def each_block(visit, j, start):
        def along(i, carry):
            visit(i, {"blocks": lax.rem(block + i, nb), "lev": j})
            return carry

        lax.fori_loop(start, nb, along, 0, unroll=unroll)

    def to_rest(visit):
        for j in range(1, nl):
            each_block(visit, j, 1)

            @pl.when(lev != j)
            def _():
                visit(0, {"blocks": block, "lev": j})

    def load(src, dst, sem):
        pltpu.make_async_copy(src, dst, in_sem.at[sem]).start()

    def load_flow():
        load(u_hbm, u_ref, 6)
        load(v_hbm, v_ref, 6)

    load(t_hbm, t_ref, 0)
    load(g_hbm, g_ref, 0)
    load(bottom_hbm, bottom_ref, 1)
    load(shave_hbm, shave_ref, 2)
    load(nbr_hbm, nbr_ref, 3)
    load(fold_hbm, fold_ref, 4)
    load(side_hbm, side_ref, 5)

    @pl.when(first_column)
    def _():
        load_flow()

    def arrived(ref, sem):
        pltpu.make_async_copy(ref, ref, in_sem.at[sem]).wait()

    barrier = pltpu.get_barrier_semaphore()

    def signal(i, device):
        pl.semaphore_signal(barrier, inc=1, device_id=device, device_id_type=MESH)

    @pl.when(first_column)
    def _():
        each_block(signal, 0, 1)

    to_rest(signal)

    lane = lax.broadcasted_iota(jnp.int32, (rows, cols), 1)
    row = lax.broadcasted_iota(jnp.int32, (rows, cols), 0)
    lane_pair = lane // 2

    blank = jnp.zeros((levels, cols), F32)

    def strip(fields):
        wide = jnp.zeros((rows, cols), F32)
        for j, field in enumerate(fields):
            wide = jnp.where(lane_pair == j, pltpu.roll(field(), 2 * j + 1, 1), wide)
        return wide.T

    def pack_edges():
        fields = [functools.partial(lambda k: t_ref[k], k) for k in range(levels)]
        fields += [functools.partial(lambda k: u_ref[k], k) for k in range(levels)]
        edge_ref[...] = strip(fields)
        t_north = t_ref[:, rows - 1, :]
        v_north = v_ref[:, rows - 1, :]
        t_edges = (
            edge_ref[pl.ds(1, levels, stride=2), :],
            edge_ref[pl.ds(0, levels, stride=2), :],
            t_ref[:, 0, :],
            t_north,
        )
        f_edges = (
            edge_ref[pl.ds(2 * levels + 1, levels, stride=2), :],
            edge_ref[pl.ds(2 * levels, levels, stride=2), :],
            v_ref[:, 0, :],
            v_north,
        )
        mirror = (
            lax.broadcasted_iota(jnp.int32, (cols, cols), 0)
            + lax.broadcasted_iota(jnp.int32, (cols, cols), 1)
            == cols - 1
        ).astype(F32)
        turned = jnp.dot(
            jnp.concatenate([t_north, v_north], 0),
            mirror,
            precision=HIGHEST,
            preferred_element_type=F32,
        )
        for s in range(4):
            own_ref[s] = t_edges[s]
            own_ref[4 + s] = f_edges[s]
        own_ref[8] = turned[:levels]
        own_ref[9] = turned[levels:]
        arrived(nbr_ref, 3)
        sides = [nbr_ref[0, s] for s in range(4)]

        def pack(i, carry):
            there = lax.rem(block + i, nb)
            t_side, f_side = blank, blank
            for s in range(4):
                hit = sides[s] == there
                t_side = jnp.where(hit, t_edges[s], t_side)
                f_side = jnp.where(hit, f_edges[s], f_side)
            pay_ref[i - 1, :levels, :] = t_side
            pay_ref[i - 1, levels : 2 * levels, :] = f_side
            pay_ref[i - 1, 2 * levels :, :] = turned
            return carry

        lax.fori_loop(1, nb, pack, 0, unroll=unroll)

    def send_edges():
        def send(i, carry):
            pltpu.make_async_remote_copy(
                src_ref=pay_ref.at[i - 1],
                dst_ref=halo_ref.at[i - 1],
                send_sem=edge_send,
                recv_sem=edge_recv,
                device_id={"blocks": lax.rem(block + i, nb), "lev": lev},
                device_id_type=MESH,
            ).start()
            return carry

        lax.fori_loop(1, nb, send, 0, unroll=unroll)

    arrived(bottom_ref, 1)
    arrived(shave_ref, 2)
    arrived(tg_ref, 0)

    @pl.when(jnp.logical_not(first_column))
    def _():
        load_flow()

    bottom = bottom_ref[...]
    shave = shave_ref[...]
    last = bottom - 1
    volume = jnp.where(bottom > 0, last.astype(F32) + shave, 0.0)
    source = jnp.clip(volume, 0.0, 1.0) * (g_ref[0] - t_ref[0])
    for k in range(1, levels):
        source += jnp.clip(volume - k, 0.0, 1.0) * (g_ref[k] - t_ref[k])
    source = RATE * jnp.sum(source, axis=0, keepdims=True)
    volume = jnp.sum(volume, axis=0, keepdims=True)
    half = cols // 2
    first_half = lax.broadcasted_iota(jnp.int32, (1, cols), 1) < half
    own_part = jnp.where(
        first_half,
        source + pltpu.roll(source, half, 1),
        volume + pltpu.roll(volume, half, 1),
    )
    part_ref[...] = own_part

    sum_ref[...] = own_part

    def send_row(src, dst, send, recv, device):
        pltpu.make_async_remote_copy(
            src_ref=src,
            dst_ref=dst,
            send_sem=send,
            recv_sem=recv,
            device_id=device,
            device_id_type=MESH,
        ).start()

    def meet():
        @pl.when(first_column)
        def _():
            pl.semaphore_wait(barrier, nb - 1)
            each_block(
                lambda i, device: send_row(
                    part_ref, column_ref.at[i - 1], part_send, column_recv, device
                ),
                0,
                1,
            )

        @pl.when(jnp.logical_not(first_column))
        def _():
            pl.semaphore_wait(barrier, n - 1)
            pl.semaphore_signal(
                ready, inc=1, device_id={"blocks": block, "lev": 0}, device_id_type=MESH
            )

            def send_part(send):
                return lambda i, device: send_row(
                    part_ref, parts_ref.at[(lev - 1) * nb + i], send, part_recv, device
                )

            each_block(send_part(part_send), 0, 0)
            to_rest(send_part(rest_send))

    @pl.when(far)
    def _():
        meet()

    load(w_hbm, w_ref, 7)
    arrived(flow_ref.at[:2], 6)
    pack_edges()

    @pl.when(jnp.logical_not(far))
    def _():
        meet()

    send_edges()

    arrived(w_ref, 7)
    arrived(fold_ref, 4)
    arrived(side_ref, 5)
    t_edges = [own_ref[s] for s in range(4)]
    f_edges = [own_ref[4 + s] for s in range(4)]
    turned_t, turned_f = own_ref[8], own_ref[9]
    sides = [nbr_ref[0, s] for s in range(4)]
    fold = fold_ref[0, 0]

    inverse = 1.0 / shave
    bottom_east = pltpu.roll(bottom, cols - 1, 1)
    open_east = jnp.where(lane == cols - 1, 0, jnp.minimum(bottom, bottom_east))
    open_north = jnp.where(row == rows - 1, 0, jnp.minimum(bottom, pltpu.roll(bottom, rows - 1, 0)))
    partner_shave = jnp.where(bottom_east == bottom, pltpu.roll(shave, cols - 1, 1), 1.0)
    scale = 1.0 / (shave + partner_shave)
    weight = shave * scale
    partner_weight = partner_shave * scale
    struck = jnp.where(shave < THIN_LIMIT, last, -1)
    struck_west = pltpu.roll(struck, 1, 1)

    edge_ref[...] = strip(
        (
            lambda: bottom.astype(F32),
            lambda: shave,
            lambda: jnp.where(lane == 0, weight, pltpu.roll(partner_weight, 1, 1)),
            lambda: jnp.where(lane == 0, struck, struck_west).astype(F32),
        )
    )

    upper = jnp.zeros((rows, cols), F32)
    for k in range(levels):
        t = t_ref[k]
        u = u_ref[k]
        v = v_ref[k]
        face = jnp.where(k < open_east, 0.5 * (u + pltpu.roll(u, cols - 1, 1)), 0.0)
        flux = upwind(face, t, pltpu.roll(t, cols - 1, 1))
        divergence = pltpu.roll(flux, 1, 1) - flux
        face = jnp.where(k < open_north, 0.5 * (v + pltpu.roll(v, rows - 1, 0)), 0.0)
        flux = upwind(face, t, pltpu.roll(t, rows - 1, 0))
        divergence += pltpu.roll(flux, 1, 0) - flux
        if k < levels - 1:
            face = jnp.where(k + 1 < bottom, 0.5 * (w_ref[k] + w_ref[k + 1]), 0.0)
            lower = upwind(face, t_ref[k + 1], t)
        else:
            lower = jnp.zeros((rows, cols), F32)
        divergence += lower - upper
        upper = lower
        x = t + divergence * jnp.where(k == last, inverse, 1.0) + RATE * (g_ref[k] - t)
        merged = weight * x + partner_weight * pltpu.roll(x, cols - 1, 1)
        x = jnp.where(struck == k, merged, x)
        x_ref[k] = jnp.where(struck_west == k, pltpu.roll(merged, 1, 1), x)

    places = (0, 1, cols - 2, cols - 1)
    kinds = len(places)
    source_row = lax.broadcasted_iota(jnp.int32, (kinds * levels, levels * cols), 0)
    target = lax.broadcasted_iota(jnp.int32, (kinds * levels, levels * cols), 1)
    chosen = jnp.zeros((kinds * levels, levels * cols), F32)
    for p, place in enumerate(places):
        chosen = jnp.where(target == (source_row - p * levels) * cols + place, 1.0, chosen)
    chosen = chosen.astype(jnp.bfloat16)
    for p in range(3):
        pick_ref[p * kinds * levels : (p + 1) * kinds * levels, :] = chosen

    grid = lax.broadcasted_iota(jnp.int32, (levels, cols), 0)
    grid_f = grid.astype(F32)
    edge_bottom = (
        edge_ref[1:2, :],
        edge_ref[0:1, :],
        bottom_ref[0:1, :].astype(F32),
        bottom_ref[rows - 1 : rows, :].astype(F32),
    )
    edge_shave = (
        edge_ref[3:4, :],
        edge_ref[2:3, :],
        shave_ref[0:1, :],
        shave_ref[rows - 1 : rows, :],
    )
    wets, scales = [], []
    for s in range(4):
        beyond = side_ref[s : s + 1, :].astype(F32)
        wets.append(grid_f < jnp.minimum(edge_bottom[s], beyond))
        scales.append(jnp.where(grid_f == edge_bottom[s] - 1.0, 1.0 / edge_shave[s], 1.0))
    side_weight = (edge_ref[5:6, :], edge_ref[4:5, :])
    side_struck = (edge_ref[7:8, :] == grid_f, edge_ref[6:7, :] == grid_f)

    found_t = [jnp.where(sides[s] == block, t_edges[s ^ 1], blank) for s in range(4)]
    found_f = [jnp.where(sides[s] == block, f_edges[s ^ 1], blank) for s in range(4)]
    hit = fold == block
    found_t[3] = jnp.where(hit, turned_t, found_t[3])
    found_f[3] = jnp.where(hit, -turned_f, found_f[3])

    @pl.when(first_column)
    def _():
        pltpu.make_async_copy(column_ref, column_ref, column_recv).wait()
        sum_ref[...] = part_ref[...] + jnp.sum(column_ref[...], axis=0)
        pl.semaphore_wait(ready, nl - 1)
        for j in range(1, nl):
            send_row(
                sum_ref,
                parts_ref.at[(j - 1) * nb],
                rest_send,
                part_recv,
                {"blocks": block, "lev": j},
            )

    pltpu.make_async_copy(halo_ref, halo_ref, edge_recv).wait()

    def collect(i, carry):
        found_t, found_f = list(carry[0]), list(carry[1])
        origin = lax.rem(block + nb - i, nb)
        side_t, side_f, over_t, over_f = (
            halo_ref[i - 1, p * levels : (p + 1) * levels, :] for p in range(4)
        )
        found_t = [jnp.where(sides[s] == origin, side_t, found_t[s]) for s in range(4)]
        found_f = [jnp.where(sides[s] == origin, side_f, found_f[s]) for s in range(4)]
        hit = fold == origin
        found_t[3] = jnp.where(hit, over_t, found_t[3])
        found_f[3] = jnp.where(hit, -over_f, found_f[3])
        return found_t, found_f

    found_t, found_f = lax.fori_loop(1, nb, collect, (found_t, found_f), unroll=unroll)

    gains = []
    for s in range(4):
        face = jnp.where(wets[s], 0.5 * (f_edges[s] + found_f[s]), 0.0)
        if s % 2 == 0:
            flux = upwind(face, found_t[s], t_edges[s])
        else:
            flux = -upwind(face, t_edges[s], found_t[s])
        gains.append(flux * scales[s])
    west = jnp.where(side_struck[0], side_weight[0] * gains[0], gains[0])
    east = jnp.where(side_struck[1], side_weight[1] * gains[1], gains[1])
    wide = jnp.concatenate(
        [
            west,
            jnp.where(side_struck[0], west, 0.0),
            jnp.where(side_struck[1], east, 0.0),
            east,
        ],
        0,
    )
    high = wide.astype(jnp.bfloat16)
    rest = wide - high.astype(F32)
    middle = rest.astype(jnp.bfloat16)
    low = (rest - middle.astype(F32)).astype(jnp.bfloat16)
    placed = lax.dot_general(
        jnp.concatenate([high, middle, low], 0),
        pick_ref[...],
        (((0,), (0,)), ((), ())),
        preferred_element_type=F32,
    )
    for k in range(levels):
        x_ref[k] += placed[:, k * cols : (k + 1) * cols]
    for s, r in ((2, 0), (3, rows - 1)):
        merged = weight[r : r + 1] * gains[s] + partner_weight[r : r + 1] * pltpu.roll(
            gains[s], cols - 1, 1
        )
        gain = jnp.where(struck[r : r + 1] == grid, merged, gains[s])
        gain = jnp.where(struck_west[r : r + 1] == grid, pltpu.roll(merged, 1, 1), gain)
        x_ref[:, r, :] += gain

    pltpu.make_async_copy(parts_ref, parts_ref, part_recv).wait()
    terms = [sum_ref[...]]
    terms += [parts_ref[i] for i in range(n - nb)] if unroll else [jnp.sum(parts_ref[...], axis=0)]
    while len(terms) > 1:
        terms = [sum(terms[i : i + 2]) for i in range(0, len(terms), 2)]
    total = terms[0]
    total_source = jnp.sum(jnp.where(first_half, total, 0.0), axis=1, keepdims=True)
    total_volume = jnp.sum(jnp.where(first_half, 0.0, total), axis=1, keepdims=True)
    mean_ref[...] = jnp.broadcast_to(total_source / total_volume, (1, cols))

    pltpu.make_async_copy(halo_ref, halo_ref, edge_send).wait()

    def sent(ref, sem):
        pltpu.make_async_copy(ref, ref, sem).wait()

    @pl.when(first_column)
    def _():
        sent(column_ref, part_send)
        sent(parts_ref.at[: nl - 1], rest_send)

    @pl.when(jnp.logical_not(first_column))
    def _():
        sent(parts_ref.at[:nb], part_send)
        sent(parts_ref.at[: n - nb - 1], rest_send)


def finish(x_ref, mean_ref, bottom_ref, out_hbm, held_ref, sem):
    levels, _, cols = x_ref.shape
    mean = mean_ref[...]
    half = x_ref.shape[1] // 2
    for k in range(levels):
        for r in (0, half):
            piece = pl.ds(r, half)
            held_ref[k, piece] = jnp.where(k < bottom_ref[piece], x_ref[k, piece] - mean, 0.0)
            pltpu.make_async_copy(held_ref.at[k, piece], out_hbm.at[k, piece], sem).start()
    pltpu.make_async_copy(held_ref, held_ref, sem).wait()


def local(
    nb,
    nl,
    tracers,
    east_velocity,
    north_velocity,
    upward_velocity,
    target,
    bottom,
    shave_fraction,
    side_bottom,
    neighbors,
    fold_partner,
    thin_pairs,
):
    levels, rows, cols = tracers.shape[2:]
    in_hbm = functools.partial(pltpu.with_memory_space_constraint, memory_space=pltpu.HBM)
    cube = (levels, rows, cols)
    n = nb * nl
    vmem = pl.BlockSpec(memory_space=pltpu.VMEM)
    grant = (14 << 20) + 4 * cols * (8 * levels * nb + 8 * n)
    anywhere = pl.BlockSpec(memory_space=pl.ANY)
    kept = pl.pallas_call(
        functools.partial(kernel, nb, nl),
        out_shape=(
            pltpu.VMEM(cube, F32),
            pltpu.VMEM((1, cols), F32),
            pltpu.VMEM((rows, cols), jnp.int32),
        ),
        in_specs=[anywhere] * 10,
        out_specs=(vmem,) * 3,
        scratch_shapes=[
            pltpu.VMEM((2, *cube), F32),
            pltpu.VMEM((3, *cube), F32),
            pltpu.VMEM((rows, cols), F32),
            pltpu.SMEM((1, 4), jnp.int32),
            pltpu.SMEM((1, 1), jnp.int32),
            pltpu.VMEM((4, cols), jnp.int32),
            pltpu.VMEM((cols, rows), F32),
            pltpu.VMEM((10, levels, cols), F32),
            pltpu.VMEM((12 * levels, levels * cols), jnp.bfloat16),
            pltpu.VMEM((nb - 1, 4 * levels, cols), F32),
            pltpu.VMEM((nb - 1, 4 * levels, cols), F32),
            pltpu.VMEM((1, cols), F32),
            pltpu.VMEM((1, cols), F32),
            pltpu.VMEM((nb - 1, 1, cols), F32),
            pltpu.VMEM((n - nb, 1, cols), F32),
            pltpu.SemaphoreType.DMA((8,)),
            pltpu.SemaphoreType.DMA,
            pltpu.SemaphoreType.DMA,
            pltpu.SemaphoreType.DMA,
            pltpu.SemaphoreType.DMA,
            pltpu.SemaphoreType.DMA,
            pltpu.SemaphoreType.DMA,
            pltpu.SemaphoreType.REGULAR,
        ],
        compiler_params=pltpu.CompilerParams(
            collective_id=0, has_side_effects=True, vmem_limit_bytes=grant
        ),
    )(
        in_hbm(neighbors),
        fold_partner.reshape(1, 1),
        in_hbm(side_bottom.reshape(4, cols)),
        in_hbm(tracers.reshape(cube)),
        in_hbm(east_velocity.reshape(cube)),
        in_hbm(north_velocity.reshape(cube)),
        in_hbm(upward_velocity.reshape(cube)),
        in_hbm(target.reshape(cube)),
        in_hbm(bottom.reshape(rows, cols)),
        in_hbm(shave_fraction.reshape(rows, cols)),
    )
    stepped = pl.pallas_call(
        finish,
        out_shape=pltpu.HBM(cube, F32),
        in_specs=[vmem] * 3,
        out_specs=anywhere,
        scratch_shapes=[pltpu.VMEM(cube, F32), pltpu.SemaphoreType.DMA],
        compiler_params=pltpu.CompilerParams(vmem_limit_bytes=2 << 20),
    )(*kept)
    return stepped.reshape(tracers.shape)


def solution(mesh):
    placed = (
        P("blocks", "lev", None, None, None),
        P("blocks", None, None, None),
        P("blocks", None, None, None),
        P("blocks", None, None, None),
        P("blocks", "lev", None, None, None),
        P("blocks", None, None),
        P("blocks", None, None),
        P("blocks", None, None),
        P("blocks", None),
        P("blocks"),
        P("blocks", None, None),
    )
    return jax.shard_map(
        functools.partial(local, mesh.shape["blocks"], mesh.shape["lev"]),
        mesh=mesh,
        in_specs=placed,
        out_specs=P("blocks", "lev", None, None, None),
        check_vma=False,
    )
```

```python
import functools

import jax
import jax.numpy as jnp
from jax import lax
from jax.experimental import pallas as pl
from jax.experimental.pallas import tpu as pltpu
from jax.sharding import PartitionSpec as P

RATE = 0.5
THIN_LIMIT = 0.35
MESH = pl.DeviceIdType.MESH
F32 = jnp.float32
HIGHEST = lax.Precision.HIGHEST


def upwind(face, first, second):
    return jnp.maximum(face, 0.0) * first + jnp.minimum(face, 0.0) * second


def kernel(
    nb,
    nl,
    nbr_hbm,
    fold_hbm,
    side_hbm,
    t_hbm,
    u_hbm,
    v_hbm,
    w_hbm,
    g_hbm,
    bottom_hbm,
    shave_hbm,
    x_ref,
    mean_ref,
    bottom_ref,
    tg_ref,
    flow_ref,
    shave_ref,
    nbr_ref,
    fold_ref,
    side_ref,
    edge_ref,
    own_ref,
    pick_ref,
    pay_ref,
    halo_ref,
    part_ref,
    sum_ref,
    rows_ref,
    in_sem,
    edge_send,
    edge_recv,
    part_send,
    column_recv,
    part_recv,
    ready,
):
    t_ref, g_ref = tg_ref.at[0], tg_ref.at[1]
    u_ref, v_ref, w_ref = (flow_ref.at[i] for i in range(3))
    levels, rows, cols = t_ref.shape
    column_ref, parts_ref = rows_ref.at[: nb - 1], rows_ref.at[nb - 1 :]
    n = nb * nl
    unroll = n <= 64
    block = lax.axis_index("blocks")
    lev = lax.axis_index("lev")
    far = block >= nb // 4

    first_column = lev == 0

    def each_block(visit, j, start):
        def along(i, carry):
            visit(i, {"blocks": lax.rem(block + i, nb), "lev": j})
            return carry

        lax.fori_loop(start, nb, along, 0, unroll=unroll)

    def to_rest(visit):
        for j in range(1, nl):
            each_block(visit, j, 1)

            @pl.when(lev != j)
            def _():
                visit(0, {"blocks": block, "lev": j})

    def load(src, dst, sem):
        pltpu.make_async_copy(src, dst, in_sem.at[sem]).start()

    def load_flow():
        load(u_hbm, u_ref, 6)
        load(v_hbm, v_ref, 6)
        load(w_hbm, w_ref, 6)

    load(g_hbm, g_ref, 0)
    load(t_hbm, t_ref, 0)
    load(bottom_hbm, bottom_ref, 1)
    load(shave_hbm, shave_ref, 2)
    load(nbr_hbm, nbr_ref, 3)
    load(fold_hbm, fold_ref, 4)
    load(side_hbm, side_ref, 5)

    @pl.when(first_column)
    def _():
        load_flow()

    def arrived(ref, sem):
        pltpu.make_async_copy(ref, ref, in_sem.at[sem]).wait()

    barrier = pltpu.get_barrier_semaphore()

    def signal(i, device):
        pl.semaphore_signal(barrier, inc=1, device_id=device, device_id_type=MESH)

    @pl.when(first_column)
    def _():
        each_block(signal, 0, 1)

    to_rest(signal)

    lane = lax.broadcasted_iota(jnp.int32, (rows, cols), 1)
    row = lax.broadcasted_iota(jnp.int32, (rows, cols), 0)
    lane_pair = lane // 2

    blank = jnp.zeros((levels, cols), F32)

    def strip(fields):
        wide = jnp.zeros((rows, cols), F32)
        for j, field in enumerate(fields):
            wide = jnp.where(lane_pair == j, pltpu.roll(field(), 2 * j + 1, 1), wide)
        return wide.T

    def pack_edges():
        fields = [functools.partial(lambda k: t_ref[k], k) for k in range(levels)]
        fields += [functools.partial(lambda k: u_ref[k], k) for k in range(levels)]
        edge_ref[...] = strip(fields)
        t_north = t_ref[:, rows - 1, :]
        v_north = v_ref[:, rows - 1, :]
        t_edges = (
            edge_ref[pl.ds(1, levels, stride=2), :],
            edge_ref[pl.ds(0, levels, stride=2), :],
            t_ref[:, 0, :],
            t_north,
        )
        f_edges = (
            edge_ref[pl.ds(2 * levels + 1, levels, stride=2), :],
            edge_ref[pl.ds(2 * levels, levels, stride=2), :],
            v_ref[:, 0, :],
            v_north,
        )
        mirror = (
            lax.broadcasted_iota(jnp.int32, (cols, cols), 0)
            + lax.broadcasted_iota(jnp.int32, (cols, cols), 1)
            == cols - 1
        ).astype(F32)
        turned = jnp.dot(
            jnp.concatenate([t_north, v_north], 0),
            mirror,
            precision=HIGHEST,
            preferred_element_type=F32,
        )
        for s in range(4):
            own_ref[s] = t_edges[s]
            own_ref[4 + s] = f_edges[s]
        own_ref[8] = turned[:levels]
        own_ref[9] = turned[levels:]
        arrived(nbr_ref, 3)
        sides = [nbr_ref[0, s] for s in range(4)]

        def pack(i, carry):
            there = lax.rem(block + i, nb)
            t_side, f_side = blank, blank
            for s in range(4):
                hit = sides[s] == there
                t_side = jnp.where(hit, t_edges[s], t_side)
                f_side = jnp.where(hit, f_edges[s], f_side)
            pay_ref[i - 1, :levels, :] = t_side
            pay_ref[i - 1, levels : 2 * levels, :] = f_side
            pay_ref[i - 1, 2 * levels :, :] = turned
            return carry

        lax.fori_loop(1, nb, pack, 0, unroll=unroll)

    def send_edges():
        def send(i, carry):
            pltpu.make_async_remote_copy(
                src_ref=pay_ref.at[i - 1],
                dst_ref=halo_ref.at[i - 1],
                send_sem=edge_send,
                recv_sem=edge_recv,
                device_id={"blocks": lax.rem(block + i, nb), "lev": lev},
                device_id_type=MESH,
            ).start()
            return carry

        lax.fori_loop(1, nb, send, 0, unroll=unroll)

    arrived(bottom_ref, 1)
    arrived(shave_ref, 2)
    arrived(tg_ref, 0)

    @pl.when(jnp.logical_not(first_column))
    def _():
        load_flow()

    bottom = bottom_ref[...]
    shave = shave_ref[...]
    last = bottom - 1
    volume = jnp.where(bottom > 0, last.astype(F32) + shave, 0.0)
    source = jnp.clip(volume, 0.0, 1.0) * (g_ref[0] - t_ref[0])
    for k in range(1, levels):
        source += jnp.clip(volume - k, 0.0, 1.0) * (g_ref[k] - t_ref[k])
    source = RATE * jnp.sum(source, axis=0, keepdims=True)
    volume = jnp.sum(volume, axis=0, keepdims=True)
    half = cols // 2
    first_half = lax.broadcasted_iota(jnp.int32, (1, cols), 1) < half
    own_part = jnp.where(
        first_half,
        source + pltpu.roll(source, half, 1),
        volume + pltpu.roll(volume, half, 1),
    )
    part_ref[...] = own_part

    sum_ref[...] = own_part

    def send_row(src, dst, send, recv, device):
        pltpu.make_async_remote_copy(
            src_ref=src,
            dst_ref=dst,
            send_sem=send,
            recv_sem=recv,
            device_id=device,
            device_id_type=MESH,
        ).start()

    def meet():
        @pl.when(first_column)
        def _():
            pl.semaphore_wait(barrier, nb - 1)
            each_block(
                lambda i, device: send_row(
                    part_ref, column_ref.at[i - 1], part_send, column_recv, device
                ),
                0,
                1,
            )

        @pl.when(jnp.logical_not(first_column))
        def _():
            pl.semaphore_wait(barrier, n - 1)
            pl.semaphore_signal(
                ready, inc=1, device_id={"blocks": block, "lev": 0}, device_id_type=MESH
            )

            def send_part(send):
                return lambda i, device: send_row(
                    part_ref, parts_ref.at[(lev - 1) * nb + i], send, part_recv, device
                )

            each_block(send_part(part_send), 0, 0)
            to_rest(send_part(part_send))

    @pl.when(far)
    def _():
        meet()

    arrived(flow_ref, 6)
    pack_edges()

    @pl.when(jnp.logical_not(far))
    def _():
        meet()

    send_edges()

    arrived(fold_ref, 4)
    arrived(side_ref, 5)
    t_edges = [own_ref[s] for s in range(4)]
    f_edges = [own_ref[4 + s] for s in range(4)]
    turned_t, turned_f = own_ref[8], own_ref[9]
    sides = [nbr_ref[0, s] for s in range(4)]
    fold = fold_ref[0, 0]

    inverse = 1.0 / shave
    bottom_east = pltpu.roll(bottom, cols - 1, 1)
    open_east = jnp.where(lane == cols - 1, 0, jnp.minimum(bottom, bottom_east))
    open_north = jnp.where(row == rows - 1, 0, jnp.minimum(bottom, pltpu.roll(bottom, rows - 1, 0)))
    partner_shave = jnp.where(bottom_east == bottom, pltpu.roll(shave, cols - 1, 1), 1.0)
    scale = 1.0 / (shave + partner_shave)
    weight = shave * scale
    partner_weight = partner_shave * scale
    struck = jnp.where(shave < THIN_LIMIT, last, -1)
    struck_west = pltpu.roll(struck, 1, 1)

    edge_ref[...] = strip(
        (
            lambda: bottom.astype(F32),
            lambda: shave,
            lambda: jnp.where(lane == 0, weight, pltpu.roll(partner_weight, 1, 1)),
            lambda: jnp.where(lane == 0, struck, struck_west).astype(F32),
        )
    )

    upper = jnp.zeros((rows, cols), F32)
    for k in range(levels):
        t = t_ref[k]
        u = u_ref[k]
        v = v_ref[k]
        face = jnp.where(k < open_east, 0.5 * (u + pltpu.roll(u, cols - 1, 1)), 0.0)
        flux = upwind(face, t, pltpu.roll(t, cols - 1, 1))
        divergence = pltpu.roll(flux, 1, 1) - flux
        face = jnp.where(k < open_north, 0.5 * (v + pltpu.roll(v, rows - 1, 0)), 0.0)
        flux = upwind(face, t, pltpu.roll(t, rows - 1, 0))
        divergence += pltpu.roll(flux, 1, 0) - flux
        if k < levels - 1:
            face = jnp.where(k + 1 < bottom, 0.5 * (w_ref[k] + w_ref[k + 1]), 0.0)
            lower = upwind(face, t_ref[k + 1], t)
        else:
            lower = jnp.zeros((rows, cols), F32)
        divergence += lower - upper
        upper = lower
        x = t + divergence * jnp.where(k == last, inverse, 1.0) + RATE * (g_ref[k] - t)
        merged = weight * x + partner_weight * pltpu.roll(x, cols - 1, 1)
        x = jnp.where(struck == k, merged, x)
        x_ref[k] = jnp.where(struck_west == k, pltpu.roll(merged, 1, 1), x)

    places = (0, 1, cols - 2, cols - 1)
    kinds = len(places)
    source_row = lax.broadcasted_iota(jnp.int32, (kinds * levels, levels * cols), 0)
    target = lax.broadcasted_iota(jnp.int32, (kinds * levels, levels * cols), 1)
    chosen = jnp.zeros((kinds * levels, levels * cols), F32)
    for p, place in enumerate(places):
        chosen = jnp.where(target == (source_row - p * levels) * cols + place, 1.0, chosen)
    chosen = chosen.astype(jnp.bfloat16)
    for p in range(3):
        pick_ref[p * kinds * levels : (p + 1) * kinds * levels, :] = chosen

    grid = lax.broadcasted_iota(jnp.int32, (levels, cols), 0)
    grid_f = grid.astype(F32)
    edge_bottom = (
        edge_ref[1:2, :],
        edge_ref[0:1, :],
        bottom_ref[0:1, :].astype(F32),
        bottom_ref[rows - 1 : rows, :].astype(F32),
    )
    edge_shave = (
        edge_ref[3:4, :],
        edge_ref[2:3, :],
        shave_ref[0:1, :],
        shave_ref[rows - 1 : rows, :],
    )
    wets, scales = [], []
    for s in range(4):
        beyond = side_ref[s : s + 1, :].astype(F32)
        wets.append(grid_f < jnp.minimum(edge_bottom[s], beyond))
        scales.append(jnp.where(grid_f == edge_bottom[s] - 1.0, 1.0 / edge_shave[s], 1.0))
    side_weight = (edge_ref[5:6, :], edge_ref[4:5, :])
    side_struck = (edge_ref[7:8, :] == grid_f, edge_ref[6:7, :] == grid_f)

    found_t = [jnp.where(sides[s] == block, t_edges[s ^ 1], blank) for s in range(4)]
    found_f = [jnp.where(sides[s] == block, f_edges[s ^ 1], blank) for s in range(4)]
    hit = fold == block
    found_t[3] = jnp.where(hit, turned_t, found_t[3])
    found_f[3] = jnp.where(hit, -turned_f, found_f[3])

    @pl.when(first_column)
    def _():
        pltpu.make_async_copy(column_ref, column_ref, column_recv).wait()
        sum_ref[...] = part_ref[...] + jnp.sum(column_ref[...], axis=0)
        pl.semaphore_wait(ready, nl - 1)
        for j in range(1, nl):
            send_row(
                sum_ref,
                parts_ref.at[(j - 1) * nb],
                part_send,
                part_recv,
                {"blocks": block, "lev": j},
            )

    pltpu.make_async_copy(halo_ref, halo_ref, edge_recv).wait()

    def collect(i, carry):
        found_t, found_f = list(carry[0]), list(carry[1])
        origin = lax.rem(block + nb - i, nb)
        side_t, side_f, over_t, over_f = (
            halo_ref[i - 1, p * levels : (p + 1) * levels, :] for p in range(4)
        )
        found_t = [jnp.where(sides[s] == origin, side_t, found_t[s]) for s in range(4)]
        found_f = [jnp.where(sides[s] == origin, side_f, found_f[s]) for s in range(4)]
        hit = fold == origin
        found_t[3] = jnp.where(hit, over_t, found_t[3])
        found_f[3] = jnp.where(hit, -over_f, found_f[3])
        return found_t, found_f

    found_t, found_f = lax.fori_loop(1, nb, collect, (found_t, found_f), unroll=unroll)

    gains = []
    for s in range(4):
        face = jnp.where(wets[s], 0.5 * (f_edges[s] + found_f[s]), 0.0)
        if s % 2 == 0:
            flux = upwind(face, found_t[s], t_edges[s])
        else:
            flux = -upwind(face, t_edges[s], found_t[s])
        gains.append(flux * scales[s])
    west = jnp.where(side_struck[0], side_weight[0] * gains[0], gains[0])
    east = jnp.where(side_struck[1], side_weight[1] * gains[1], gains[1])
    wide = jnp.concatenate(
        [
            west,
            jnp.where(side_struck[0], west, 0.0),
            jnp.where(side_struck[1], east, 0.0),
            east,
        ],
        0,
    )
    high = wide.astype(jnp.bfloat16)
    rest = wide - high.astype(F32)
    middle = rest.astype(jnp.bfloat16)
    low = (rest - middle.astype(F32)).astype(jnp.bfloat16)
    placed = lax.dot_general(
        jnp.concatenate([high, middle, low], 0),
        pick_ref[...],
        (((0,), (0,)), ((), ())),
        preferred_element_type=F32,
    )
    for k in range(levels):
        x_ref[k] += placed[:, k * cols : (k + 1) * cols]
    for s, r in ((2, 0), (3, rows - 1)):
        merged = weight[r : r + 1] * gains[s] + partner_weight[r : r + 1] * pltpu.roll(
            gains[s], cols - 1, 1
        )
        gain = jnp.where(struck[r : r + 1] == grid, merged, gains[s])
        gain = jnp.where(struck_west[r : r + 1] == grid, pltpu.roll(merged, 1, 1), gain)
        x_ref[:, r, :] += gain

    pltpu.make_async_copy(parts_ref, parts_ref, part_recv).wait()
    terms = [sum_ref[...]]
    terms += [parts_ref[i] for i in range(n - nb)] if unroll else [jnp.sum(parts_ref[...], axis=0)]
    while len(terms) > 1:
        terms = [sum(terms[i : i + 2]) for i in range(0, len(terms), 2)]
    total = terms[0]
    total_source = jnp.sum(jnp.where(first_half, total, 0.0), axis=1, keepdims=True)
    total_volume = jnp.sum(jnp.where(first_half, 0.0, total), axis=1, keepdims=True)
    mean_ref[...] = jnp.broadcast_to(total_source / total_volume, (1, cols))

    pltpu.make_async_copy(halo_ref, halo_ref, edge_send).wait()

    def sent(ref, sem):
        pltpu.make_async_copy(ref, ref, sem).wait()

    @pl.when(first_column)
    def _():
        sent(rows_ref.at[: nb + nl - 2], part_send)

    @pl.when(jnp.logical_not(first_column))
    def _():
        sent(rows_ref, part_send)


def finish(x_ref, mean_ref, bottom_ref, out_hbm, held_ref, sem):
    levels, _, cols = x_ref.shape
    mean = mean_ref[...]
    half = x_ref.shape[1] // 2
    for k in range(levels):
        for r in (0, half):
            piece = pl.ds(r, half)
            held_ref[k, piece] = jnp.where(k < bottom_ref[piece], x_ref[k, piece] - mean, 0.0)
            pltpu.make_async_copy(held_ref.at[k, piece], out_hbm.at[k, piece], sem).start()
    pltpu.make_async_copy(held_ref, held_ref, sem).wait()


def local(
    nb,
    nl,
    tracers,
    east_velocity,
    north_velocity,
    upward_velocity,
    target,
    bottom,
    shave_fraction,
    side_bottom,
    neighbors,
    fold_partner,
    thin_pairs,
):
    levels, rows, cols = tracers.shape[2:]
    in_hbm = functools.partial(pltpu.with_memory_space_constraint, memory_space=pltpu.HBM)
    cube = (levels, rows, cols)
    n = nb * nl
    vmem = pl.BlockSpec(memory_space=pltpu.VMEM)
    grant = (14 << 20) + 4 * cols * (8 * levels * nb + 8 * n)
    anywhere = pl.BlockSpec(memory_space=pl.ANY)
    kept = pl.pallas_call(
        functools.partial(kernel, nb, nl),
        out_shape=(
            pltpu.VMEM(cube, F32),
            pltpu.VMEM((1, cols), F32),
            pltpu.VMEM((rows, cols), jnp.int32),
        ),
        in_specs=[anywhere] * 10,
        out_specs=(vmem,) * 3,
        scratch_shapes=[
            pltpu.VMEM((2, *cube), F32),
            pltpu.VMEM((3, *cube), F32),
            pltpu.VMEM((rows, cols), F32),
            pltpu.SMEM((1, 4), jnp.int32),
            pltpu.SMEM((1, 1), jnp.int32),
            pltpu.VMEM((4, cols), jnp.int32),
            pltpu.VMEM((cols, rows), F32),
            pltpu.VMEM((10, levels, cols), F32),
            pltpu.VMEM((12 * levels, levels * cols), jnp.bfloat16),
            pltpu.VMEM((nb - 1, 4 * levels, cols), F32),
            pltpu.VMEM((nb - 1, 4 * levels, cols), F32),
            pltpu.VMEM((1, cols), F32),
            pltpu.VMEM((1, cols), F32),
            pltpu.VMEM((n - 1, 1, cols), F32),
            pltpu.SemaphoreType.DMA((7,)),
            pltpu.SemaphoreType.DMA,
            pltpu.SemaphoreType.DMA,
            pltpu.SemaphoreType.DMA,
            pltpu.SemaphoreType.DMA,
            pltpu.SemaphoreType.DMA,
            pltpu.SemaphoreType.REGULAR,
        ],
        compiler_params=pltpu.CompilerParams(
            collective_id=0, has_side_effects=True, vmem_limit_bytes=grant
        ),
    )(
        in_hbm(neighbors),
        fold_partner.reshape(1, 1),
        in_hbm(side_bottom.reshape(4, cols)),
        in_hbm(tracers.reshape(cube)),
        in_hbm(east_velocity.reshape(cube)),
        in_hbm(north_velocity.reshape(cube)),
        in_hbm(upward_velocity.reshape(cube)),
        in_hbm(target.reshape(cube)),
        in_hbm(bottom.reshape(rows, cols)),
        in_hbm(shave_fraction.reshape(rows, cols)),
    )
    stepped = pl.pallas_call(
        finish,
        out_shape=pltpu.HBM(cube, F32),
        in_specs=[vmem] * 3,
        out_specs=anywhere,
        scratch_shapes=[pltpu.VMEM(cube, F32), pltpu.SemaphoreType.DMA],
        compiler_params=pltpu.CompilerParams(vmem_limit_bytes=2 << 20),
    )(*kept)
    return stepped.reshape(tracers.shape)


def solution(mesh):
    placed = (
        P("blocks", "lev", None, None, None),
        P("blocks", None, None, None),
        P("blocks", None, None, None),
        P("blocks", None, None, None),
        P("blocks", "lev", None, None, None),
        P("blocks", None, None),
        P("blocks", None, None),
        P("blocks", None, None),
        P("blocks", None),
        P("blocks"),
        P("blocks", None, None),
    )
    return jax.shard_map(
        functools.partial(local, mesh.shape["blocks"], mesh.shape["lev"]),
        mesh=mesh,
        in_specs=placed,
        out_specs=P("blocks", "lev", None, None, None),
        check_vma=False,
    )
```
